128 devices in a mesh: dom: 16 (over x, y), grp: 8 (over z, core).
Axes of the slice: x: 4, y: 4, z: 4, core: 2. Of those that a mesh axis runs over, the one named last changes fastest.
Arguments:
- valence: float32 [128, 64, 1024], P('dom', None, 'grp')
- start_potential: float32 [128, 64, 1024], P('dom', None, 'grp'), may hold values from -3 to 3
- atom_tiles: float32 [32768, 512], P(('dom', 'grp')), may hold values from -12 to 12
- atom_home: int32 [32768, 1], P(('dom', 'grp')), may hold values from 0 to 127; in each aligned block of 256 rows (0 to 255, 256 to 511, ...) at most 4 rows name the same one
- atom_offset_x: int32 [32768, 1], P(('dom', 'grp')), may hold values from 0 to 7
- atom_offset_y: int32 [32768, 1], P(('dom', 'grp')), may hold values from 0 to 63
- atom_offset_z: int32 [32768, 1], P(('dom', 'grp')), may hold values from 0 to 120
- atom_size: int32 [32768, 1], P(('dom', 'grp')), may hold values from 4 to 8
Outputs:
- potential: float32 [128, 64, 1024], P('dom', None, 'grp')
- stress: float32 [6], replicated
The draws below stay inside these ranges and needn't reach their ends.
Inputs may be any that keep to these rules, and one draw needn't show every extreme that they name: `atom_home`: at most 4 atoms among the rows of one device share a home, and some home has exactly 4 of them.
All inputs are finite; a program needn't handle non-finite values.
Results may differ from the reference program's by a relative error of at most 0.00014.
Values sent between devices are 32-bit elements; how exact they have to be, the bound alone decides.
No kernel may reach another device: no remote copies, remote signals or barrier semaphores. Data moves between devices by JAX's collectives and lax.ppermute only.
A program may use at most 128 MiB of HBM per device.

```python
import math
import jax
import jax.numpy as jnp
import numpy as np
from jax import lax

CX = 8
CY = 64
CZ = 128
ATOMS_DEV = 256
TE = 8
NU = 2
TE3 = 512
CAP = 4
ATOMS = 32768
NX = 128
NZ = 1024
N_GRP = 8
DEVICES = 128


def draw_valence(key, part):
    position_x = jnp.arange(NX, dtype=jnp.float32) / NX
    growth = (1.0 + 2.0 * position_x)[:, None, None]
    rough_part = jnp.clip(jax.random.normal(key, (NX, CY, NZ), jnp.float32), -5.0, 5.0)
    return rough_part * growth


def set_ends(values, rng, least, high):
    extent = values.shape
    place = [jax.random.randint(jax.random.fold_in(rng, axis), (), 0, extent[axis]) for axis in range(len(extent))]
    values = values.at[tuple(place)].set(least)
    longest = extent.index(max(extent))
    place[longest] = (place[longest] + 1) % extent[longest]
    return values.at[tuple(place)].set(high)


def shard_levels(key, dims, pieces, smallest, top_value):
    def one(axis_at, parts):
        steps = jax.random.uniform(jax.random.fold_in(jax.random.fold_in(key, 6), axis_at), (parts,), jnp.float32, smallest / len(pieces), top_value / len(pieces))
        return jnp.repeat(jnp.exp(steps), dims[axis_at] // parts).reshape((-1,) + (1,) * (len(dims) - axis_at - 1))

    factor_of = one(*pieces[0])
    for cut in pieces[1:]:
        factor_of = factor_of * one(*cut)
    return factor_of


def routed_block(rng, own, number, rows, number_of, top, most, skew):
    sequence = jax.random.permutation(rng, number_of)
    crowded, usual = shares(number_of, rows * top, most, skew, True), shares(number_of, rows * top, most, skew, False)
    places = jnp.arange(number_of)

    def named(lengths, offset_by):
        used = int((lengths > 0).sum())
        fixed = max(1, used // 4)
        passed = fixed + (places - fixed + offset_by * (used - fixed)) % max(1, number_of - fixed)
        return jnp.zeros((number_of,), jnp.int32).at[sequence[jnp.where(places < fixed, places, passed)]].set(jnp.asarray(lengths, jnp.int32))

    lengths = jnp.where(number % 4 == 0, named(crowded, number // 4), named(usual, number - number // 4 - 1))
    mixed = jax.random.permutation(jax.random.fold_in(own, 3), number_of)
    donor, receiver = mixed[0:number_of // 2 * 2:2], mixed[1:number_of // 2 * 2:2]
    room = jnp.minimum(lengths[donor] - 1, most - lengths[receiver]) // 2
    room = jnp.where((donor == sequence[0]) | (receiver == sequence[0]) | (lengths[receiver] == 0), 0, jnp.maximum(room, 0))
    passed = jax.random.randint(jax.random.fold_in(own, 4), (number_of // 2,), 0, 1 << 20) % (room + 1)
    lengths = lengths.at[donor].add(-passed).at[receiver].add(passed)
    items = jnp.searchsorted(jnp.cumsum(lengths), jnp.arange(rows * top), side="right").astype(jnp.int32)
    table = items.reshape(top, rows).T
    table = table[jax.random.permutation(jax.random.fold_in(own, 1), rows)]
    offset_by = jax.random.randint(jax.random.fold_in(own, 2), (rows, 1), 0, top)
    return jnp.take_along_axis(table, (jnp.arange(top)[None, :] + offset_by) % top, axis=1)


def shares(count, total, most, slope, full):
    loads = [(1 << 20) // math.isqrt(rank ** slope) + 1 for rank in range(1, count + 1)]
    largest = most if full else min(most, max(-(-total // count), total * loads[0] // sum(loads)))
    least = 1 if total - largest >= count - 1 else 0
    counts, surplus = [largest] + [least] * (count - 1), total - largest - least * (count - 1)
    while surplus > 0:
        candidates = [i for i in range(1, count) if counts[i] < largest] or [i for i in range(1, count) if counts[i] < most]
        mass, budget = sum([loads[i] for i in candidates]), surplus
        for i in candidates:
            extra = min(most - counts[i], max(1, budget * loads[i] // mass), surplus)
            counts[i] = counts[i] + extra
            surplus = surplus - extra
    return np.array(counts)


def scatter_about(own_key, extent, scale, bound, cuts=(), kind=jnp.bfloat16):
    drawn = jax.random.normal(own_key, extent, jnp.float32) * scale
    if len(cuts) > 0:
        drawn = shard_levels(own_key, extent, cuts, -0.22, 0.18) * drawn
    return jnp.clip(drawn, min=-bound, max=bound).astype(kind)


def setup_inputs(seed: int = 0) -> dict:
    arg_keys = jax.random.split(jax.random.key(seed), 9)
    valence = draw_valence(jax.random.fold_in(arg_keys[8], 71), 0)
    start_potential = scatter_about(arg_keys[1], (NX, CY, NZ), 0.5, 3.0, ((0, 16), (2, 8)), jnp.float32)
    atom_tiles = scatter_about(arg_keys[2], (ATOMS, TE3), 2.0, 12.0, ((0, 128),), jnp.float32)
    atom_home_keys = jax.random.split(jax.random.fold_in(arg_keys[3], 1), ATOMS // ATOMS_DEV)
    atom_home_turns = jax.random.permutation(jax.random.fold_in(arg_keys[3], 3), ATOMS // ATOMS_DEV)
    atom_home = jax.vmap(lambda own, number: routed_block(jax.random.fold_in(arg_keys[3], 2), own, number, ATOMS_DEV, DEVICES, 1, CAP, 2))(atom_home_keys, atom_home_turns).reshape((ATOMS, 1))
    atom_offset_x = set_ends(jax.random.randint(arg_keys[4], (ATOMS, 1), 0, CX), jax.random.fold_in(arg_keys[4], 1), 0, CX - 1).astype(jnp.int32)
    atom_offset_y = set_ends(jax.random.randint(arg_keys[5], (ATOMS, 1), 0, CY), jax.random.fold_in(arg_keys[5], 1), 0, CY - 1).astype(jnp.int32)
    atom_offset_z = set_ends(jax.random.randint(arg_keys[6], (ATOMS, 1), 0, CZ - TE + 1), jax.random.fold_in(arg_keys[6], 1), 0, CZ - TE).astype(jnp.int32)
    atom_size = set_ends(jax.random.randint(arg_keys[7], (ATOMS, 1), TE // 2, TE + 1), jax.random.fold_in(arg_keys[7], 1), TE // 2, TE).astype(jnp.int32)
    return {"valence": valence, "start_potential": start_potential, "atom_tiles": atom_tiles, "atom_home": atom_home, "atom_offset_x": atom_offset_x, "atom_offset_y": atom_offset_y, "atom_offset_z": atom_offset_z, "atom_size": atom_size}


DAMPING = 2.0 / 3.0

def sine_basis(length_now):
    steps_now = jnp.arange(length_now, dtype=jnp.float32)
    table = jnp.sqrt(2.0 / (length_now + 1)) * jnp.sin(jnp.pi * (steps_now[:, None] + 1.0) * (steps_now[None, :] + 1.0) / (length_now + 1))
    values = 2.0 - 2.0 * jnp.cos(jnp.pi * (steps_now + 1.0) / (length_now + 1))
    return (table, values)

def cyclic_basis(length_now):
    steps_now = jnp.arange(length_now, dtype=jnp.float32)[:, None]
    column = jnp.arange(length_now, dtype=jnp.int32)[None, :]
    freqs = ((column + 1) // 2).astype(jnp.float32)
    angles = 2.0 * jnp.pi * freqs * steps_now / length_now
    use_sine = (column % 2 == 0) & (column > 0)
    edge_cols = (column == 0) | (column == length_now - 1)
    scales = jnp.where(edge_cols, jnp.sqrt(1.0 / length_now), jnp.sqrt(2.0 / length_now))
    table = scales * jnp.where(use_sine, jnp.sin(angles), jnp.cos(angles))
    values = 2.0 - 2.0 * jnp.cos(2.0 * jnp.pi * freqs[0] / length_now)
    return (table, values)

def exact_solve(source, spacing_sq):
    table_x, values_x = sine_basis(source.shape[0])
    table_y, values_y = cyclic_basis(source.shape[1])
    table_z, values_z = sine_basis(source.shape[2])
    highest = lax.Precision.HIGHEST
    modes = jnp.einsum('ia,ijk->ajk', table_x, source, precision=highest)
    modes = jnp.einsum('jb,ajk->abk', table_y, modes, precision=highest)
    modes = jnp.einsum('kc,abk->abc', table_z, modes, precision=highest)
    modes = modes * spacing_sq / (values_x[:, None, None] + values_y[None, :, None] + values_z[None, None, :])
    result = jnp.einsum('kc,abc->abk', table_z, modes, precision=highest)
    result = jnp.einsum('jb,abk->ajk', table_y, result, precision=highest)
    return jnp.einsum('ia,ajk->ijk', table_x, result, precision=highest)

def operate(current, spacing_sq):
    padded = jnp.pad(current, ((1, 1), (0, 0), (1, 1)))
    beside = padded[2:, :, 1:-1] + padded[:-2, :, 1:-1]
    beside = beside + jnp.roll(current, 1, axis=1) + jnp.roll(current, -1, axis=1)
    beside = beside + padded[1:-1, :, 2:] + padded[1:-1, :, :-2]
    return (6.0 * current - beside) / spacing_sq

def smooth(current, source, spacing_sq, sweeps):
    for step_index in range(sweeps):
        if current is None:
            current = DAMPING * spacing_sq / 6.0 * source
        else:
            current = current + DAMPING * spacing_sq / 6.0 * (source - operate(current, spacing_sq))
    return current

def restrict(residue):
    dims_now = residue.shape
    coarse = residue.reshape(dims_now[0] // 2, 2, dims_now[1] // 2, 2, dims_now[2] // 2, 2)
    return coarse.mean(axis=(1, 3, 5))

def prolong(correction):
    dims_now = correction.shape
    spread = jnp.broadcast_to(correction[:, None, :, None, :, None], (dims_now[0], 2, dims_now[1], 2, dims_now[2], 2))
    return spread.reshape(dims_now[0] * 2, dims_now[1] * 2, dims_now[2] * 2)

def vcycle(level_index, current, source):
    spacing_sq = 4.0 ** level_index
    if level_index == 3:
        return exact_solve(source, spacing_sq)
    current = smooth(current, source, spacing_sq, NU)
    residue = source - operate(current, spacing_sq)
    correction = vcycle(level_index + 1, None, restrict(residue))
    current = current + prolong(correction)
    return smooth(current, source, spacing_sq, NU)

def reference(valence, start_potential, atom_tiles, atom_home, atom_offset_x, atom_offset_y, atom_offset_z, atom_size):
    tile_index = jnp.arange(TE, dtype=jnp.int32)
    inside = tile_index[None, :] < atom_size
    inside_cube = inside[:, :, None, None] & inside[:, None, :, None] & inside[:, None, None, :]
    masked = atom_tiles * inside_cube.reshape(atom_tiles.shape).astype(jnp.float32)
    home_device = atom_home[:, 0]
    corner_x = home_device // N_GRP * CX + atom_offset_x[:, 0]
    corner_z = home_device % N_GRP * CZ + atom_offset_z[:, 0]
    cells_x = corner_x[:, None] + tile_index[None, :]
    cells_y = (atom_offset_y[:, 0][:, None] + tile_index[None, :]) % CY
    cells_z = corner_z[:, None] + tile_index[None, :]
    atom_count = atom_tiles.shape[0]
    tile_shape = (atom_count, TE, TE, TE)
    index_x = jnp.broadcast_to(cells_x[:, :, None, None], tile_shape)
    index_y = jnp.broadcast_to(cells_y[:, None, :, None], tile_shape)
    index_z = jnp.broadcast_to(cells_z[:, None, None, :], tile_shape)
    compensation = jnp.zeros(valence.shape, jnp.float32).at[index_x, index_y, index_z].add(masked.reshape(tile_shape), mode='drop')
    density = valence + compensation
    potential = vcycle(0, start_potential, density)
    padded = jnp.pad(potential, ((1, 1), (0, 0), (1, 1)))
    grad_x = 0.5 * (padded[2:, :, 1:-1] - padded[:-2, :, 1:-1])
    grad_y = 0.5 * (jnp.roll(potential, -1, axis=1) - jnp.roll(potential, 1, axis=1))
    grad_z = 0.5 * (padded[1:-1, :, 2:] - padded[1:-1, :, :-2])
    totals = jnp.stack([jnp.sum(grad_x * grad_x), jnp.sum(grad_y * grad_y), jnp.sum(grad_z * grad_z), jnp.sum(grad_y * grad_z), jnp.sum(grad_x * grad_z), jnp.sum(grad_x * grad_y), jnp.sum(potential * density)])
    cell_count = potential.shape[0] * potential.shape[1] * potential.shape[2]
    products = totals[:6] / cell_count
    energy = 0.5 * totals[6] / cell_count
    diagonal_mask = jnp.array([1.0, 1.0, 1.0, 0.0, 0.0, 0.0], jnp.float32)
    stress = products - energy * diagonal_mask
    return (potential, stress)
```

```python
import functools

import jax
import jax.numpy as jnp
import numpy as np
from jax import lax
from jax.experimental import pallas as pl
from jax.experimental.pallas import tpu as pltpu
from jax.sharding import Mesh
from jax.sharding import PartitionSpec as P

TE = 8
CAP = 4
DOM = ("dom_0", "dom_1")
GRP = ("grp_0", "grp_1")
ALL = DOM + GRP
F32 = jnp.float32
I32 = jnp.int32
HI = lax.Precision.HIGHEST
VM = pl.BlockSpec(memory_space=pltpu.VMEM)
SM = pl.BlockSpec(memory_space=pltpu.SMEM)

CX, CY, CZ = 8, 64, 128
NDOM, NGRP = 16, 8
NDEV = NDOM * NGRP
ATOMS = 256
TILE_ROWS = 4
LANES = 128
MSG = CAP * TILE_ROWS * LANES + LANES
PAR = pltpu.CompilerParams(vmem_limit_bytes=48 * 1024 * 1024)


def sds(*shape, dtype=F32):
    return jax.ShapeDtypeStruct(shape, dtype)


def lanes_of(shape):
    return lax.broadcasted_iota(I32, shape, len(shape) - 1)


def rows_of(shape):
    return lax.broadcasted_iota(I32, shape, len(shape) - 2)


def dot(a, b):
    return lax.dot_general(
        a, b, (((1,), (0,)), ((), ())), precision=HI, preferred_element_type=F32
    )


def pack_kernel(scal, tiles, out, rows, slots, corners, count):
    corners[...] = jnp.zeros_like(corners)
    for r in range(TILE_ROWS):
        for g in range(ATOMS // 8):
            rows[pl.ds(g * 8 * TILE_ROWS + r, 8, stride=TILE_ROWS), :] = tiles[
                g * 8 : g * 8 + 8, r * LANES : (r + 1) * LANES
            ]

    def clear(i, c):
        count[i] = 0
        return c

    lax.fori_loop(0, NDEV, clear, 0, unroll=8)
    lane = lanes_of((1, LANES))

    def one(n, c):
        home = scal[n]
        rank = count[home]
        count[home] = rank + 1
        slots[pl.ds(home * (CAP * TILE_ROWS) + rank * TILE_ROWS, TILE_ROWS), :] = rows[
            pl.ds(n * TILE_ROWS, TILE_ROWS), :
        ]
        first = rank * 4
        old = corners[pl.ds(home, 1), :]
        for i in range(4):
            value = scal[ATOMS * (i + 1) + n].astype(F32)
            old = jnp.where(lane == first + i, value, old)
        corners[pl.ds(home, 1), :] = old
        return c

    lax.fori_loop(0, ATOMS, one, 0, unroll=4)
    for g in range(NDEV // 8):
        for j in range(CAP * TILE_ROWS):
            out[g * 8 : g * 8 + 8, j * LANES : (j + 1) * LANES] = slots[
                pl.ds(g * 8 * CAP * TILE_ROWS + j, 8, stride=CAP * TILE_ROWS), :
            ]
    out[:, CAP * TILE_ROWS * LANES :] = corners[...]


def pack_atoms(scal, tiles):
    return pl.pallas_call(
        pack_kernel,
        out_shape=sds(NDEV, MSG),
        in_specs=[SM, VM],
        out_specs=VM,
        scratch_shapes=[
            pltpu.VMEM((ATOMS * TILE_ROWS, LANES), F32),
            pltpu.VMEM((NDEV * CAP * TILE_ROWS, LANES), F32),
            pltpu.VMEM((NDEV, LANES), F32),
            pltpu.SMEM((NDEV,), I32),
        ],
        compiler_params=PAR,
        name="pack_atoms",
    )(scal, tiles)


ZB = CZ // 8 + 1
YB = 4


def deposit_kernel(got, grid, up2, down, tiles, acc, corner_v, corner_s, sem):
    corner_v[...] = got[:, CAP * TILE_ROWS * LANES :].astype(I32)
    copy = pltpu.make_async_copy(corner_v, corner_s, sem)
    copy.start()
    def spread(g, c):
        for k in range(CAP):
            for r in range(TILE_ROWS):
                j = k * TILE_ROWS + r
                col = got[pl.ds(pl.multiple_of(g * 8, 8), 8), j * LANES : (j + 1) * LANES]
                base = g * 8 * CAP * TE + k * TE + 2 * r
                tiles[pl.ds(base, 8, stride=CAP * TE), :] = col
                tiles[pl.ds(base + 1, 8, stride=CAP * TE), :] = pltpu.roll(col, 64, 1)
        return c

    lax.fori_loop(0, NDEV // 8, spread, 0)

    def clear(i, c):
        acc[pl.ds(pl.multiple_of(i * 16, 16), 16), :] = jnp.zeros((16, LANES), F32)
        return c

    lax.fori_loop(0, YB * ZB, clear, 0, unroll=4)
    copy.wait()
    lane = lanes_of((8, LANES))
    tile_a = rows_of((8, LANES))
    tile_b = lane // 8
    tile_c = lane % 8
    need = jnp.maximum(jnp.maximum(tile_a, tile_b), tile_c)
    need = jnp.where(lane < 64, need, 99)

    def one(src, c):
        for k in range(CAP):
            ox = corner_s[src, 4 * k]
            oy = corner_s[src, 4 * k + 1]
            oz = corner_s[src, 4 * k + 2]
            size = corner_s[src, 4 * k + 3]
            value = tiles[pl.ds(pl.multiple_of((src * CAP + k) * TE, 8), TE), :]
            value = jnp.where(need < size, value, 0.0)
            z_in, z_block = oz & 7, oz >> 3
            y_in, y_block = oy & 15, oy >> 4
            near = jnp.where(tile_c < 8 - z_in, value, 0.0)
            far = jnp.where(tile_c < 8 - z_in, 0.0, value)
            shift = y_in * 8 + z_in
            near = pltpu.roll(near, shift, 1)
            far = pltpu.roll(far, (shift + 120) & 127, 1)
            same = lane >= y_in * 8
            row = (y_block * ZB + z_block) * 16 + ox
            wrapped = (((y_block + 1) & 3) * ZB + z_block) * 16 + ox
            acc[pl.ds(row, 8), :] += jnp.where(same, near, 0.0)
            acc[pl.ds(row + 16, 8), :] += jnp.where(same, far, 0.0)
            acc[pl.ds(wrapped, 8), :] += jnp.where(same, 0.0, near)
            acc[pl.ds(wrapped + 16, 8), :] += jnp.where(same, 0.0, far)
        return c

    lax.fori_loop(0, NDEV, one, 0)
    group = lane // 8

    def lay_out(yb, c):
        for xg in range(2):
            blocks = [
                acc[pl.ds(pl.multiple_of((yb * ZB + zb) * 16 + xg * 8, 8), 8), :]
                for zb in range(CZ // 8)
            ]
            for yy in range(16):
                row = jnp.zeros((8, LANES), F32)
                for zb in range(CZ // 8):
                    moved = pltpu.roll(blocks[zb], (8 * zb - 8 * yy) % 128, 1)
                    row = jnp.where(group == zb, moved, row)
                grid[pl.ds(xg * 8 * CY + yb * 16 + yy, 8, stride=CY), :] = row
        return c

    lax.fori_loop(0, YB, lay_out, 0)
    up2[...] = grid[10 * CY : 15 * CY, :]
    down[...] = grid[0 : 6 * CY, :]


def deposit(got):
    return pl.pallas_call(
        deposit_kernel,
        out_shape=(sds(16 * CY, LANES), sds(5 * CY, LANES), sds(6 * CY, LANES)),
        in_specs=[VM],
        out_specs=(VM, VM, VM),
        scratch_shapes=[
            pltpu.VMEM((NDEV * CAP * TE, LANES), F32),
            pltpu.VMEM((YB * ZB * 16, LANES), F32),
            pltpu.VMEM((NDEV, LANES), I32),
            pltpu.SMEM((NDEV, LANES), I32),
            pltpu.SemaphoreType.DMA,
        ],
        compiler_params=PAR,
        name="deposit",
    )(got)


HU, HF = 7, 6
NU_, NF = CX + 2 * HU, CX + 2 * HF
PACKED = NU_ + NF
ZGROUPS = -(-PACKED // 8)


def join_kernel(grid, from1, from2, above, valence, v_lo, v_hi, start, u_lo, u_hi, f, u, left, right):
    u[0:HU] = u_lo[...]
    u[HU : HU + CX] = start[...]
    u[HU + CX :] = u_hi[...]
    for p in range(NF):
        x = p - HF
        if x < 0:
            total = v_lo[p] + from1[x + 6]
            if x < -1:
                total = total + from2[x + 6]
        elif x < CX:
            total = valence[x] + grid[x * CY : (x + 1) * CY, :]
            if x < 7:
                total = total + from1[x + 6]
        else:
            total = v_hi[x - CX] + above[x - CX]
            if x < 15:
                total = total + grid[x * CY : (x + 1) * CY, :]
        f[p] = total
    slot = lanes_of((CY, LANES)) // 16
    for g in range(ZGROUPS):
        lo = jnp.zeros((CY, LANES), F32)
        hi = jnp.zeros((CY, LANES), F32)
        for k in range(8):
            p = g * 8 + k
            if p < PACKED:
                plane = u[p] if p < NU_ else f[p - NU_]
                lo = jnp.where(slot == k, pltpu.roll(plane, (16 * k) % 128, 1) if k else plane, lo)
                shift = (16 * k - 112) % 128
                hi = jnp.where(slot == k, pltpu.roll(plane, shift, 1) if shift else plane, hi)
        left[g] = lo
        right[g] = hi


def join(*args):
    return pl.pallas_call(
        join_kernel,
        out_shape=(
            sds(NF, CY, LANES),
            sds(NU_, CY, LANES),
            sds(ZGROUPS, CY, LANES),
            sds(ZGROUPS, CY, LANES),
        ),
        in_specs=[VM] * 10,
        out_specs=(VM,) * 4,
        compiler_params=PAR,
        name="join",
    )(*args)


W0 = 256
X1, Y1, Z1 = 4, 32, 64
X2, Y2, Z2 = 2, 16, 32


def beside(ref, p):
    c = ref[p]
    n, w = c.shape
    return c, (
        ref[p + 1]
        + ref[p - 1]
        + (pltpu.roll(c, 1, 0) + pltpu.roll(c, n - 1, 0))
        + (pltpu.roll(c, 1, 1) + pltpu.roll(c, w - 1, 1))
    )


def z_mask(width, own, grp, total):
    lane = lanes_of((1, width))
    split = own + (width - own) // 2
    z = grp * own + jnp.where(lane < split, lane, lane - width)
    return ((z >= 0) & (z < total)).astype(F32)


def x_ok(x, total):
    return jnp.where((x >= 0) & (x < total), 1.0, 0.0).astype(F32)


def halves(n):
    r = lax.broadcasted_iota(I32, (n, 2 * n), 0)
    c = lax.broadcasted_iota(I32, (n, 2 * n), 1)
    return ((c // 2) == r).astype(F32)


def doubles(n):
    r = lax.broadcasted_iota(I32, (2 * n, n), 0)
    c = lax.broadcasted_iota(I32, (2 * n, n), 1)
    return ((r // 2) == c).astype(F32)


def lane_halves(n):
    r = lax.broadcasted_iota(I32, (2 * n, n), 0)
    c = lax.broadcasted_iota(I32, (2 * n, n), 1)
    return ((r // 2) == c).astype(F32)


def before_kernel(place, f_in, u_in, from_left, from_right, u2, f, f1, chunk, u, ua, ub, pairs, v1, r1):
    dom, grp = place[0], place[1]
    lane = lanes_of((CY, LANES))
    for p in range(PACKED):
        g, k = p // 8, p % 8
        right = from_right[g]
        right = pltpu.roll(right, (-16 * k) % 128, 1) if k else right
        left = from_left[g]
        shift = (112 - 16 * k) % 128
        left = pltpu.roll(left, shift, 1) if shift else left
        edge = jnp.where(lane < 16, right, jnp.where(lane >= 112, left, 0.0))
        if p < NU_:
            u[p, :, 0:LANES] = u_in[p]
            u[p, :, LANES:] = edge
        else:
            f[p - NU_, :, 0:LANES] = f_in[p - NU_]
            f[p - NU_, :, LANES:] = edge
    mask = z_mask(W0, CZ, grp, NGRP * CZ)

    def sweep1(p, c):
        centre, around = beside(u, p + 1)
        new = (3.0 * centre + around + f[p]) * (1.0 / 9.0)
        ua[p] = new * (mask * x_ok(dom * CX + p - HF, NDOM * CX))
        return c

    lax.fori_loop(0, NF, sweep1, 0)

    def sweep2(p, c):
        centre, around = beside(ua, p + 1)
        new = (3.0 * centre + around + f[p + 1]) * (1.0 / 9.0)
        u2[p] = new * (mask * x_ok(dom * CX + p - 5, NDOM * CX))
        return c

    lax.fori_loop(0, NF - 2, sweep2, 0)

    def residue0(q, c):
        total = None
        for i in range(2):
            p = 2 * q + i + 1
            centre, around = beside(u2, p)
            r = f[p + 1] - (6.0 * centre - around)
            total = r if total is None else total + r
        pairs[pl.ds(pl.multiple_of(q * CY, CY), CY), :] = total
        return c

    lax.fori_loop(0, 8, residue0, 0)
    summed = dot(pairs[...], lane_halves(LANES))
    half_y = halves(Y1) * 0.125
    mask1 = z_mask(LANES, Z1, grp, NGRP * Z1)
    for q in range(8):
        part = dot(half_y, summed[q * CY : (q + 1) * CY, :])
        f1[q] = part * (mask1 * x_ok(dom * X1 + q - 2, NDOM * X1))
    for q in range(8):
        v1[q] = f1[q] * (4.0 / 9.0)
    for q in range(1, 7):
        centre, around = beside(v1, q)
        new = (3.0 * centre + around + 4.0 * f1[q]) * (1.0 / 9.0)
        r1[q] = new * (mask1 * x_ok(dom * X1 + q - 2, NDOM * X1))
    half_y2 = halves(Y2) * 0.125
    lane_half = lane_halves(LANES // 2)
    rows = []
    for i in range(2):
        total = None
        for j in range(2):
            q = 2 + 2 * i + j
            centre, around = beside(r1, q)
            r = f1[q] - (6.0 * centre - around) * 0.25
            total = r if total is None else total + r
        rows.append(total)
    both = dot(jnp.concatenate(rows, axis=0), jnp.concatenate([lane_half, jnp.zeros_like(lane_half)], axis=1))
    packed = jnp.zeros((8, LANES), F32)
    slot = lanes_of((8, LANES)) // 32
    for i in range(2):
        part = dot(half_y2, both[i * Y1 : (i + 1) * Y1, :])
        for yb in range(2):
            s = 2 * i + yb
            piece = part[yb * 8 : yb * 8 + 8, :]
            piece = pltpu.roll(piece, 32 * s, 1) if s else piece
            packed = jnp.where(slot == s, piece, packed)

    def spread(d, c):
        chunk[d] = packed
        return c

    lax.fori_loop(0, NDEV, spread, 0, unroll=8)


def before(place, f, u, from_left, from_right):
    return pl.pallas_call(
        before_kernel,
        out_shape=(
            sds(NF - 2, CY, W0),
            sds(NF, CY, W0),
            sds(8, Y1, LANES),
            sds(NDEV, 8, LANES),
        ),
        in_specs=[SM, VM, VM, VM, VM],
        out_specs=(VM,) * 4,
        scratch_shapes=[
            pltpu.VMEM((NU_, CY, W0), F32),
            pltpu.VMEM((NF, CY, W0), F32),
            pltpu.VMEM((8, LANES), F32),
            pltpu.VMEM((8 * CY, W0), F32),
            pltpu.VMEM((8, Y1, LANES), F32),
            pltpu.VMEM((8, Y1, LANES), F32),
        ],
        compiler_params=PAR,
        name="before",
    )(place, f, u, from_left, from_right)


NX2, NZ2 = NDOM * X2, NGRP * Z2
NX3, NY3, NZ3 = NX2 // 2, Y2 // 2, NZ2 // 2
PAD2 = 4


def tables():
    def sine(n):
        k = np.arange(n) + 1.0
        t = np.sqrt(2.0 / (n + 1)) * np.sin(np.pi * np.outer(k, k) / (n + 1))
        return t, 2.0 - 2.0 * np.cos(np.pi * k / (n + 1))

    def cyclic(n):
        j = np.arange(n)[:, None]
        col = np.arange(n)[None, :]
        freq = (col + 1) // 2
        angle = 2.0 * np.pi * freq * j / n
        use_sine = (col % 2 == 0) & (col > 0)
        edge = (col == 0) | (col == n - 1)
        t = np.where(edge, np.sqrt(1.0 / n), np.sqrt(2.0 / n)) * np.where(
            use_sine, np.sin(angle), np.cos(angle)
        )
        return t, 2.0 - 2.0 * np.cos(2.0 * np.pi * freq[0] / n)

    tx, lx = sine(NX3)
    ty, ly = cyclic(NY3)
    tz, lz = sine(NZ3)
    txy = np.kron(tx, ty)
    lxy = (lx[:, None] + ly[None, :]).reshape(-1)
    scale = 64.0 / (lxy[:, None] + lz[None, :])
    return tuple(np.asarray(a, np.float32) for a in (txy, np.ascontiguousarray(txy.T), tz, scale))


def after_kernel(
    place, got, txy, txy_t, tz, scale, f1_own, f1_lo, f1_hi, u2, f,
    potential, totals, g, w, r, f3, e, e2, a1, b1, f1, ext, s1,
):
    dom, grp = place[0], place[1]
    zero2 = jnp.zeros((Y2, NZ2), F32)
    for p in range(PAD2):
        g[p] = zero2
        g[PAD2 + NX2 + p] = zero2
        w[p] = zero2
        w[PAD2 + NX2 + p] = zero2
        r[p] = zero2
        r[PAD2 + NX2 + p] = zero2
    slot = lanes_of((8, LANES)) // 32

    def gather(d, c):
        for i in range(2):
            for yb in range(2):
                s = 2 * i + yb
                for t in range(2):
                    row = None
                    for q in range(4):
                        piece = got[d * NGRP + 4 * t + q]
                        shift = (32 * (q - s)) % 128
                        piece = pltpu.roll(piece, shift, 1) if shift else piece
                        row = piece if row is None else jnp.where(slot == q, piece, row)
                    g[PAD2 + 2 * d + i, yb * 8 : yb * 8 + 8, t * LANES : (t + 1) * LANES] = row
        return c

    lax.fori_loop(0, NDOM, gather, 0)
    lane2 = lanes_of((1, NZ2))
    not_first = (lane2 > 0).astype(F32)
    not_last = (lane2 < NZ2 - 1).astype(F32)

    def beside2(ref, p):
        c = ref[p]
        around = (
            ref[p + 1]
            + ref[p - 1]
            + (pltpu.roll(c, 1, 0) + pltpu.roll(c, Y2 - 1, 0))
            + (pltpu.roll(c, 1, 1) * not_first + pltpu.roll(c, NZ2 - 1, 1) * not_last)
        )
        return c, around

    def start2(p, c):
        w[PAD2 + p] = g[PAD2 + p] * (16.0 / 9.0)
        return c

    lax.fori_loop(0, NX2, start2, 0)

    def sweep2(p, c):
        centre, around = beside2(w, PAD2 + p)
        r[PAD2 + p] = (3.0 * centre + around + 16.0 * g[PAD2 + p]) * (1.0 / 9.0)
        return c

    lax.fori_loop(0, NX2, sweep2, 0)

    def residue2(q, c):
        total = None
        for i in range(2):
            p = PAD2 + 2 * q + i
            centre, around = beside2(r, p)
            res = g[p] - (6.0 * centre - around) * (1.0 / 16.0)
            total = res if total is None else total + res
        f3[pl.ds(pl.multiple_of(q * Y2, Y2), Y2), :] = total
        return c

    lax.fori_loop(0, NX3, residue2, 0)
    z_sums = dot(f3[...], lane_halves(NZ3))
    n3 = NX3 * NY3
    ri = lax.broadcasted_iota(I32, (n3, 2 * n3), 0)
    ci = lax.broadcasted_iota(I32, (n3, 2 * n3), 1)
    source = dot(((ci // 2) == ri).astype(F32) * 0.125, z_sums)
    modes = dot(dot(txy_t[...], source), tz[...]) * scale[...]
    solved = dot(txy[...], dot(modes, tz[...]))
    rr = lax.broadcasted_iota(I32, (NZ3, NZ2), 0)
    cc = lax.broadcasted_iota(I32, (NZ3, NZ2), 1)
    wide = dot(solved, ((cc // 2) == rr).astype(F32))
    tall = dot(((lax.broadcasted_iota(I32, (2 * n3, n3), 0) // 2) == lax.broadcasted_iota(I32, (2 * n3, n3), 1)).astype(F32), wide)
    f3[...] = tall

    def add_coarse(q, c):
        for i in range(2):
            p = PAD2 + 2 * q + i
            r[p] = r[p] + f3[pl.ds(pl.multiple_of(q * Y2, Y2), Y2), :]
        return c

    lax.fori_loop(0, NX3, add_coarse, 0)
    first2 = 2 * dom

    def post2(src, dst, n, skip):
        for p in range(n):
            q = first2 + skip + p
            centre, around = beside2(src, q)
            new = (3.0 * centre + around + 16.0 * g[q]) * (1.0 / 9.0)
            dst[q] = new * x_ok(q - PAD2, NX2)

    post2(r, w, 8, 1)
    post2(w, r, 6, 2)
    lane = lanes_of((NZ2, LANES))
    signed = jnp.where(lane < 96, lane, lane - LANES)
    place_z = ((grp * Z1 + signed + 2 * NZ2) // 2 - NZ2 == rows_of((NZ2, LANES))).astype(F32)
    double_y = doubles(Y2)
    f1[0:3] = f1_lo[...]
    f1[3:11] = f1_own[...]
    f1[11:14] = f1_hi[...]
    mask1 = z_mask(LANES, Z1, grp, NGRP * Z1)

    def ok1(p):
        return mask1 * x_ok(dom * X1 + p - 5, NDOM * X1)

    for p in range(14):
        b1[p] = f1[p] * (4.0 / 9.0)
    fine = []
    for p in range(6):
        level2 = dot(r[first2 + 2 + p], place_z)
        fine.append(dot(double_y, level2))
    for p in range(1, 13):
        centre, around = beside(b1, p)
        new = (3.0 * centre + around + 4.0 * f1[p]) * (1.0 / 9.0)
        a1[p] = new * ok1(p) + fine[(p - 1) // 2] * mask1
    for p in range(2, 12):
        centre, around = beside(a1, p)
        b1[p] = (3.0 * centre + around + 4.0 * f1[p]) * (1.0 / 9.0) * ok1(p)
    for p in range(3, 11):
        centre, around = beside(b1, p)
        s1[(p - 3) * Y1 : (p - 2) * Y1, :] = (
            (3.0 * centre + around + 4.0 * f1[p]) * (1.0 / 9.0) * ok1(p)
        )
    r0 = lax.broadcasted_iota(I32, (LANES, W0), 0)
    c0 = lax.broadcasted_iota(I32, (LANES, W0), 1)
    spread0 = dot(s1[...], ((c0 // 2) == r0).astype(F32))
    double_y0 = doubles(Y1)
    for q in range(8):
        ext[q] = dot(double_y0, spread0[q * Y1 : (q + 1) * Y1, :])
    mask = z_mask(W0, CZ, grp, NGRP * CZ)

    def add_fine(p, c):
        e[p] = u2[p + 2] + ext[(p + 1) // 2] * mask
        return c

    lax.fori_loop(0, 14, add_fine, 0)

    def last1(p, c):
        centre, around = beside(e, p + 1)
        new = (3.0 * centre + around + f[p + 4]) * (1.0 / 9.0)
        e2[p] = new * (mask * x_ok(dom * CX + p - 2, NDOM * CX))
        return c

    lax.fori_loop(0, 12, last1, 0)

    def last2(p, c):
        centre, around = beside(e2, p + 1)
        new = (3.0 * centre + around + f[p + 5]) * (1.0 / 9.0)
        e[p] = new * (mask * x_ok(dom * CX + p - 1, NDOM * CX))
        return c

    lax.fori_loop(0, 10, last2, 0)

    def sums(x, carry):
        p = x + 1
        c = e[p]
        own = c[:, 0:LANES]
        potential[x] = own
        gx = 0.5 * (e[p + 1, :, 0:LANES] - e[p - 1, :, 0:LANES])
        gy = 0.5 * (pltpu.roll(own, CY - 1, 0) - pltpu.roll(own, 1, 0))
        gz = 0.5 * (pltpu.roll(c, W0 - 1, 1) - pltpu.roll(c, 1, 1))[:, 0:LANES]
        density = f[x + 6, :, 0:LANES]
        new = (gx * gx, gy * gy, gz * gz, gy * gz, gx * gz, gx * gy, own * density)
        return tuple(
            s + jnp.sum(v.reshape(8, 8, LANES), axis=0) for s, v in zip(carry, new)
        )

    zero = jnp.zeros((8, LANES), F32)
    parts = lax.fori_loop(0, CX, sums, (zero,) * 7)
    lane8 = lanes_of((1, LANES))
    line = jnp.zeros((1, LANES), F32)
    for i, part in enumerate(parts):
        line = jnp.where(lane8 == i, jnp.sum(part), line)
    totals[...] = jnp.broadcast_to(line, (NDEV, LANES))


def after(place, got, f1_own, f1_lo, f1_hi, u2, f):
    consts = [jnp.asarray(t) for t in tables()]
    return pl.pallas_call(
        after_kernel,
        out_shape=(sds(CX, CY, CZ), sds(NDEV, LANES)),
        in_specs=[SM] + [VM] * 10,
        out_specs=(VM, VM),
        scratch_shapes=[
            pltpu.VMEM((NX2 + 2 * PAD2, Y2, NZ2), F32),
            pltpu.VMEM((NX2 + 2 * PAD2, Y2, NZ2), F32),
            pltpu.VMEM((NX2 + 2 * PAD2, Y2, NZ2), F32),
            pltpu.VMEM((NX3 * Y2, NZ2), F32),
            pltpu.VMEM((14, CY, W0), F32),
            pltpu.VMEM((12, CY, W0), F32),
            pltpu.VMEM((14, Y1, LANES), F32),
            pltpu.VMEM((14, Y1, LANES), F32),
            pltpu.VMEM((14, Y1, LANES), F32),
            pltpu.VMEM((8, CY, W0), F32),
            pltpu.VMEM((8 * Y1, LANES), F32),
        ],
        input_output_aliases={},
        compiler_params=PAR,
        name="after",
    )(place, got, *consts, f1_own, f1_lo, f1_hi, u2, f)


def stress_kernel(got, out):
    total = jnp.sum(got[...], axis=0, keepdims=True)
    lane = lanes_of((1, LANES))
    energy = jnp.sum(jnp.where(lane == 6, total, 0.0))
    cells = float(NDOM * CX * CY * NGRP * CZ)
    out[...] = total / cells - jnp.where(lane < 3, 0.5 * energy / cells, 0.0)


def stress_of(got):
    return pl.pallas_call(
        stress_kernel,
        out_shape=sds(1, LANES),
        in_specs=[VM],
        out_specs=VM,
        name="stress",
    )(got)


def shift(value, axis, distance):
    n = lax.axis_size(axis)
    route = [(i, i + distance) for i in range(n) if 0 <= i + distance < n]
    return lax.ppermute(value, axis, route)


def shards(valence, start, tiles, home, ox, oy, oz, size):
    place = jnp.stack([lax.axis_index(DOM), lax.axis_index(GRP)]).astype(I32)
    scal = jnp.concatenate([v.reshape(-1) for v in (home, ox, oy, oz, size)])
    message = pack_atoms(scal, tiles)
    got = lax.all_to_all(message, ALL, 0, 0, tiled=True)
    lower = shift(jnp.concatenate([start[CX - HU :], valence[CX - HF :]]), DOM, 1)
    upper = shift(jnp.concatenate([start[:HU], valence[:HF]]), DOM, -1)
    grid, up2, down = deposit(got)
    from1 = shift(grid[2 * CY : 15 * CY].reshape(13, CY, LANES), DOM, 1)
    from2 = shift(up2.reshape(5, CY, LANES), DOM, 2)
    above = shift(down.reshape(6, CY, LANES), DOM, -1)
    f, u, left, right = join(
        grid, from1, from2, above, valence, lower[HU:], upper[HU:], start, lower[:HU], upper[:HU]
    )
    from_right = shift(left, GRP, -1)
    from_left = shift(right, GRP, 1)
    u2, fe, f1, chunk = before(place, f, u, from_left, from_right)
    everything = lax.all_to_all(chunk, ALL, 0, 0, tiled=True)
    f1_lo = shift(f1[1:4], DOM, 1)
    f1_hi = shift(f1[4:7], DOM, -1)
    potential, totals = after(place, everything, f1, f1_lo, f1_hi, u2, fe)
    sums = lax.all_to_all(totals, ALL, 0, 0, tiled=True)
    return potential, stress_of(sums)[0, :6]


def solution(mesh):
    split = Mesh(mesh.devices.reshape(4, 4, 4, 2), ("dom_0", "dom_1", "grp_0", "grp_1"))
    atoms = P(DOM + GRP, None)
    return jax.shard_map(
        shards,
        mesh=split,
        in_specs=(P(DOM, None, GRP), P(DOM, None, GRP)) + (atoms,) * 6,
        out_specs=(P(DOM, None, GRP), P()),
        check_vma=False,
    )
```

```python
import functools

import jax
import jax.numpy as jnp
import numpy as np
from jax import lax
from jax.experimental import pallas as pl
from jax.experimental.pallas import tpu as pltpu
from jax.sharding import Mesh
from jax.sharding import PartitionSpec as P


CAP = 4
DOM = ("dom_0", "dom_1")
GRP = ("grp_0", "grp_1")
ALL = DOM + GRP
F32 = jnp.float32
I32 = jnp.int32
HI = lax.Precision.HIGHEST
VM = pl.BlockSpec(memory_space=pltpu.VMEM)
SM = pl.BlockSpec(memory_space=pltpu.SMEM)

CX, CY, CZ = 8, 64, 128
NDOM, NGRP = 16, 8
NDEV = NDOM * NGRP
ATOMS = 256
TILE_ROWS = 4
LANES = 128
PAR = pltpu.CompilerParams(vmem_limit_bytes=16 * 1024 * 1024)


def sds(*shape, dtype=F32):
    return jax.ShapeDtypeStruct(shape, dtype)


def lanes_of(shape):
    return lax.broadcasted_iota(I32, shape, len(shape) - 1)


def rows_of(shape):
    return lax.broadcasted_iota(I32, shape, len(shape) - 2)


def dot(a, b):
    return lax.dot_general(
        a, b, (((1,), (0,)), ((), ())), precision=HI, preferred_element_type=F32
    )


def dot_right(a, ones):
    hi = a.astype(jnp.bfloat16)
    lo = (a - hi.astype(F32)).astype(jnp.bfloat16)
    ones = ones.astype(jnp.bfloat16)
    return jnp.dot(hi, ones, preferred_element_type=F32) + jnp.dot(
        lo, ones, preferred_element_type=F32
    )


def dot_left(ones, a):
    hi = a.astype(jnp.bfloat16)
    lo = (a - hi.astype(F32)).astype(jnp.bfloat16)
    ones = ones.astype(jnp.bfloat16)
    return jnp.dot(ones, hi, preferred_element_type=F32) + jnp.dot(
        ones, lo, preferred_element_type=F32
    )


ROWS = CAP * TILE_ROWS + 1


def pack_kernel(
    home_h, ox_h, oy_h, oz_h, size_h, tiles_h, out, rows, count, home, ox, oy, oz, size, tiles, sem
):
    copies = [
        pltpu.make_async_copy(src, dst, sem.at[i])
        for i, (src, dst) in enumerate(
            ((home_h, home), (ox_h, ox), (oy_h, oy), (oz_h, oz), (size_h, size), (tiles_h, tiles))
        )
    ]
    for copy in copies:
        copy.start()

    def clear_out(i, c):
        out[pl.ds(pl.multiple_of(i * 8, 8), 8), :] = jnp.zeros((8, LANES), F32)
        return c

    lax.fori_loop(0, NDEV * ROWS // 8, clear_out, 0, unroll=8)

    def clear(i, c):
        count[i] = 0
        return c

    lax.fori_loop(0, NDEV, clear, 0, unroll=8)
    copies[5].wait()
    lower = lanes_of((8, LANES)) < 64
    for g in range(ATOMS // 8):
        old = [tiles[g * 8 : g * 8 + 8, r * LANES : (r + 1) * LANES] for r in range(4)]
        turned = [pltpu.roll(v, 64, 1) for v in old]
        new = (
            jnp.where(lower, old[0], turned[2]),
            jnp.where(lower, turned[0], old[2]),
            jnp.where(lower, old[1], turned[3]),
            jnp.where(lower, turned[1], old[3]),
        )
        for r in range(TILE_ROWS):
            rows[pl.ds(g * 8 * TILE_ROWS + r, 8, stride=TILE_ROWS), :] = new[r]

    for copy in copies[:5]:
        copy.wait()
    lane = lanes_of((TILE_ROWS, LANES))
    need = rows_of((TILE_ROWS, LANES)) + jnp.where(lane < 64, 0, 4)
    need = jnp.maximum(jnp.maximum(need, (lane // 8) % 8), lane % 8)
    tile_c = lane % 8
    lane1 = lanes_of((1, LANES))

    def several(step, c):
        placed = []
        for i in range(PER_STEP):
            n = step * PER_STEP + i
            z_in, y_in = oz[n] & 7, oy[n] & 15
            value = rows[pl.ds(pl.multiple_of(n * TILE_ROWS, 4), TILE_ROWS), :]
            value = jnp.where(need < size[n], value, 0.0)
            shift = y_in * 8 + z_in
            near = pltpu.roll(value, shift & 127, 1)
            far = pltpu.roll(value, (shift + 120) & 127, 1)
            placed.append(jnp.where(tile_c >= z_in, near, far))
        for i in range(PER_STEP):
            n = step * PER_STEP + i
            to = home[n]
            rank = count[to]
            count[to] = rank + 1
            base = to * ROWS
            out[pl.ds(base + rank * TILE_ROWS, TILE_ROWS), :] = placed[i]
            y_block, z_block = oy[n] >> 4, oz[n] >> 3
            row = (y_block * ZB + z_block) * 16 + ox[n]
            wrapped = (((y_block + 1) & 3) * ZB + z_block) * 16 + ox[n]
            line = jnp.where(lane1 & 3 == 0, row, wrapped)
            line = jnp.where(lane1 & 3 == 2, (oy[n] & 15) * 8, line)
            line = jnp.where(lane1 & 3 == 3, oz[n] & 7, line)
            pltpu.store(
                out.at[pl.ds(base + ROWS - 1, 1), :],
                line.astype(F32),
                mask=(lane1 >> 2) == rank,
            )
        return c

    lax.fori_loop(0, ATOMS // PER_STEP, several, 0)


PER_STEP = 16


def pack_atoms(scalars, tiles):
    return pl.pallas_call(
        pack_kernel,
        out_shape=sds(NDEV * ROWS, LANES),
        in_specs=[pl.BlockSpec(memory_space=pl.ANY)] * 6,
        out_specs=VM,
        scratch_shapes=[
            pltpu.VMEM((ATOMS * TILE_ROWS, LANES), F32),
            pltpu.SMEM((NDEV,), I32),
        ]
        + [pltpu.SMEM((ATOMS,), I32)] * 5
        + [pltpu.VMEM((ATOMS, TILE_ROWS * LANES), F32), pltpu.SemaphoreType.DMA((6,))],
        name="pack_atoms",
    )(*scalars, tiles)


ZB = CZ // 8 + 1
YB = 4


def deposit_kernel(got, valence, grid, up2, down, acc_a, acc_b, other, corner_v, corner_s, sem):
    for g in range(NDEV // 8):
        corner_v[g * 8 : g * 8 + 8, :] = got[
            pl.ds(g * 8 * ROWS + ROWS - 1, 8, stride=ROWS), :
        ].astype(I32)
    copy = pltpu.make_async_copy(corner_v, corner_s, sem)
    copy.start()

    def turn(i, c):
        at = pl.ds(pl.multiple_of(i * 32, 8), 32)
        other[at, :] = pltpu.roll(got[at, :], 64, 1)
        return c

    lax.fori_loop(0, NDEV * ROWS // 32, turn, 0, unroll=4)

    def clear(i, c):
        zero = jnp.zeros((16, LANES), F32)
        acc_a[pl.ds(pl.multiple_of(i * 16, 16), 16), :] = zero
        acc_b[pl.ds(pl.multiple_of(i * 16, 16), 16), :] = zero
        return c

    lax.fori_loop(0, YB * ZB, clear, 0, unroll=4)
    copy.wait()
    lane = lanes_of((8, LANES))
    z_of = lane % 8

    def one(src, c):
        for k in range(CAP):
            acc = acc_a if k % 2 == 0 else acc_b
            row = corner_s[src, 4 * k]
            wrapped = corner_s[src, 4 * k + 1]
            first = corner_s[src, 4 * k + 2]
            z_in = corner_s[src, 4 * k + 3]
            at = pl.ds(src * ROWS + k * TILE_ROWS, TILE_ROWS)
            value = jnp.concatenate([got[at, :], other[at, :]], axis=0)
            same = (lane >= first) & (lane < first + 64)
            here = jnp.where(same, value, 0.0)
            round_ = jnp.where(lane < first - 64, value, 0.0)
            near = z_of >= z_in
            a0 = acc[pl.ds(row, 8), :]
            a1 = acc[pl.ds(row + 16, 8), :]
            a2 = acc[pl.ds(wrapped, 8), :]
            a3 = acc[pl.ds(wrapped + 16, 8), :]
            acc[pl.ds(row, 8), :] = a0 + jnp.where(near, here, 0.0)
            acc[pl.ds(row + 16, 8), :] = a1 + jnp.where(near, 0.0, here)
            acc[pl.ds(wrapped, 8), :] = a2 + jnp.where(near, round_, 0.0)
            acc[pl.ds(wrapped + 16, 8), :] = a3 + jnp.where(near, 0.0, round_)
        return c

    lax.fori_loop(0, NDEV, one, 0)
    group = lane // 8

    def lay_out(yb, c):
        for xg in range(2):
            blocks = []
            for zb in range(CZ // 8):
                at = pl.ds(pl.multiple_of((yb * ZB + zb) * 16 + xg * 8, 8), 8)
                blocks.append(acc_a[at, :] + acc_b[at, :])
            for s in (8, 4, 2, 1):
                low = (group & s) == 0
                for i in range(16):
                    if i & s == 0:
                        one_, two = blocks[i], blocks[i + s]
                        blocks[i] = jnp.where(low, one_, pltpu.roll(two, 8 * s, 1))
                        blocks[i + s] = jnp.where(low, pltpu.roll(one_, 128 - 8 * s, 1), two)
            for yy in range(16):
                grid[pl.ds(xg * 8 * CY + yb * 16 + yy, 8, stride=CY), :] = blocks[yy]
        return c

    lax.fori_loop(0, YB, lay_out, 0)
    grid[0 : CX * CY, :] += valence[...]
    up2[...] = grid[10 * CY : 15 * CY, :]
    down[...] = grid[0 : 6 * CY, :]


def deposit(got, valence):
    return pl.pallas_call(
        deposit_kernel,
        out_shape=(sds(16 * CY, LANES), sds(5 * CY, LANES), sds(6 * CY, LANES)),
        in_specs=[VM, VM],
        out_specs=(VM, VM, VM),
        scratch_shapes=[
            pltpu.VMEM((YB * ZB * 16, LANES), F32),
            pltpu.VMEM((YB * ZB * 16, LANES), F32),
            pltpu.VMEM((NDEV * ROWS, LANES), F32),
            pltpu.VMEM((NDEV, LANES), I32),
            pltpu.SMEM((NDEV, LANES), I32),
            pltpu.SemaphoreType.DMA,
        ],
        compiler_params=PAR,
        name="deposit",
    )(got, valence.reshape(CX * CY, LANES))


HU, HF = 7, 6
NU_, NF = CX + 2 * HU, CX + 2 * HF
UGROUPS, FGROUPS = -(-NU_ // 8), -(-NF // 8)
ZGROUPS = UGROUPS + FGROUPS


def u_plane(p, u_lo, start, u_hi):
    if p < HU:
        return u_lo[p]
    return start[p - HU] if p < HU + CX else u_hi[p - HU - CX]


def pack_edges(planes, left, right, at):
    slot = lanes_of((CY, LANES)) // 16
    for g in range(-(-len(planes) // 8)):
        lo = jnp.zeros((CY, LANES), F32)
        hi = jnp.zeros((CY, LANES), F32)
        for k, plane in enumerate(planes[g * 8 : g * 8 + 8]):
            plane = plane()
            lo = jnp.where(slot == k, pltpu.roll(plane, 16 * k, 1) if k else plane, lo)
            shift_ = (16 * k - 112) % 128
            hi = jnp.where(slot == k, pltpu.roll(plane, shift_, 1) if shift_ else plane, hi)
        left[at + g] = lo
        right[at + g] = hi


def edges_kernel(start, u_lo, u_hi, left, right):
    pack_edges(
        [functools.partial(u_plane, p, u_lo, start, u_hi) for p in range(NU_)], left, right, 0
    )


def edges(start, u_lo, u_hi):
    return pl.pallas_call(
        edges_kernel,
        out_shape=(sds(UGROUPS, CY, LANES),) * 2,
        in_specs=[VM] * 3,
        out_specs=(VM,) * 2,
        compiler_params=PAR,
        name="edges",
    )(start, u_lo, u_hi)


def join_kernel(grid, from1, from2, above, u_left, u_right, f, left, right):
    left[0:UGROUPS] = u_left[...]
    right[0:UGROUPS] = u_right[...]
    for p in range(NF):
        x = p - HF
        if x < 0:
            total = from1[x + 6]
            if x < -1:
                total = total + from2[x + 6]
        elif x < CX:
            total = grid[x * CY : (x + 1) * CY, :]
            if x < 7:
                total = total + from1[x + 6]
        else:
            total = above[x - CX]
            if x < 15:
                total = total + grid[x * CY : (x + 1) * CY, :]
        f[p] = total
    pack_edges([functools.partial(lambda q: f[q], p) for p in range(NF)], left, right, UGROUPS)


def join(*args):
    return pl.pallas_call(
        join_kernel,
        out_shape=(
            sds(NF, CY, LANES),
            sds(ZGROUPS, CY, LANES),
            sds(ZGROUPS, CY, LANES),
        ),
        in_specs=[VM] * 6,
        out_specs=(VM,) * 3,
        compiler_params=PAR,
        name="join",
    )(*args)


W0 = 256
X1, Y1, Z1 = 4, 32, 64
X2, Y2, Z2 = 2, 16, 32


def beside(ref, p):
    c = ref[p]
    n, w = c.shape
    return c, (
        ref[p + 1]
        + ref[p - 1]
        + (pltpu.roll(c, 1, 0) + pltpu.roll(c, n - 1, 0))
        + (pltpu.roll(c, 1, 1) + pltpu.roll(c, w - 1, 1))
    )


def z_mask(width, own, grp, total):
    lane = lanes_of((1, width))
    split = own + (width - own) // 2
    z = grp * own + jnp.where(lane < split, lane, lane - width)
    return ((z >= 0) & (z < total)).astype(F32)


def x_ok(x, total):
    return jnp.where((x >= 0) & (x < total), 1.0, 0.0).astype(F32)


def halves(n):
    r = lax.broadcasted_iota(I32, (n, 2 * n), 0)
    c = lax.broadcasted_iota(I32, (n, 2 * n), 1)
    return ((c // 2) == r).astype(F32)


def doubles(n):
    r = lax.broadcasted_iota(I32, (2 * n, n), 0)
    c = lax.broadcasted_iota(I32, (2 * n, n), 1)
    return ((r // 2) == c).astype(F32)


def lane_halves(n):
    r = lax.broadcasted_iota(I32, (2 * n, n), 0)
    c = lax.broadcasted_iota(I32, (2 * n, n), 1)
    return ((r // 2) == c).astype(F32)


def before_kernel(
    place, f_in, u_lo, start, u_hi, from_left, from_right, u_out, f_out, f1, chunk, u, ua, f, u2, pairs, v1, r1
):
    dom, grp = place[0], place[1]
    lane = lanes_of((CY, LANES))
    for p in range(NU_ + NF):
        g, k = (p // 8, p % 8) if p < NU_ else (UGROUPS + (p - NU_) // 8, (p - NU_) % 8)
        right = from_right[g]
        right = pltpu.roll(right, (-16 * k) % 128, 1) if k else right
        left = from_left[g]
        shift = (112 - 16 * k) % 128
        left = pltpu.roll(left, shift, 1) if shift else left
        edge = jnp.where(lane < 16, right, jnp.where(lane >= 112, left, 0.0))
        if p < NU_:
            u[p, :, 0:LANES] = u_plane(p, u_lo, start, u_hi)
            u[p, :, LANES:] = edge
        else:
            f[p - NU_, :, 0:LANES] = f_in[p - NU_]
            f[p - NU_, :, LANES:] = edge
    mask = z_mask(W0, CZ, grp, NGRP * CZ)

    def sweep1(p, c):
        centre, around = beside(u, p + 1)
        new = (3.0 * centre + around + f[p]) * (1.0 / 9.0)
        ua[p] = new * (mask * x_ok(dom * CX + p - HF, NDOM * CX))
        return c

    lax.fori_loop(0, NF, sweep1, 0, unroll=4)

    def sweep2(p, c):
        centre, around = beside(ua, p + 1)
        new = (3.0 * centre + around + f[p + 1]) * (1.0 / 9.0)
        u2[p] = new * (mask * x_ok(dom * CX + p - 5, NDOM * CX))
        return c

    lax.fori_loop(0, NF - 2, sweep2, 0, unroll=3)

    u_out[...] = u2[2:16]
    f_out[...] = f[4:16]

    def residue0(q, c):
        total = None
        for i in range(2):
            p = 2 * q + i + 1
            centre, around = beside(u2, p)
            r = f[p + 1] - (6.0 * centre - around)
            total = r if total is None else total + r
        pairs[pl.ds(pl.multiple_of(q * CY, CY), CY), :] = total
        return c

    lax.fori_loop(0, 8, residue0, 0, unroll=2)
    summed = dot_right(pairs[...], lane_halves(LANES))
    half_y = halves(Y1) * 0.125
    mask1 = z_mask(LANES, Z1, grp, NGRP * Z1)
    for q in range(8):
        part = dot_left(half_y, summed[q * CY : (q + 1) * CY, :])
        f1[q] = part * (mask1 * x_ok(dom * X1 + q - 2, NDOM * X1))
    for q in range(8):
        v1[q] = f1[q] * (4.0 / 9.0)
    for q in range(1, 7):
        centre, around = beside(v1, q)
        new = (3.0 * centre + around + 4.0 * f1[q]) * (1.0 / 9.0)
        r1[q] = new * (mask1 * x_ok(dom * X1 + q - 2, NDOM * X1))
    half_y2 = halves(Y2) * 0.125
    lane_half = lane_halves(LANES // 2)
    rows = []
    for i in range(2):
        total = None
        for j in range(2):
            q = 2 + 2 * i + j
            centre, around = beside(r1, q)
            r = f1[q] - (6.0 * centre - around) * 0.25
            total = r if total is None else total + r
        rows.append(total)
    both = dot_right(jnp.concatenate(rows, axis=0), jnp.concatenate([lane_half, jnp.zeros_like(lane_half)], axis=1))
    packed = jnp.zeros((8, LANES), F32)
    slot = lanes_of((8, LANES)) // 32
    for i in range(2):
        part = dot_left(half_y2, both[i * Y1 : (i + 1) * Y1, :])
        for yb in range(2):
            s = 2 * i + yb
            piece = part[yb * 8 : yb * 8 + 8, :]
            piece = pltpu.roll(piece, 32 * s, 1) if s else piece
            packed = jnp.where(slot == s, piece, packed)

    def spread(d, c):
        chunk[d] = packed
        return c

    lax.fori_loop(0, NDEV, spread, 0, unroll=8)


def before(place, f, u_lo, start, u_hi, from_left, from_right):
    return pl.pallas_call(
        before_kernel,
        out_shape=(
            sds(14, CY, W0),
            sds(12, CY, W0),
            sds(8, Y1, LANES),
            sds(NDEV, 8, LANES),
        ),
        in_specs=[SM] + [VM] * 6,
        out_specs=(VM,) * 4,
        scratch_shapes=[
            pltpu.VMEM((NU_, CY, W0), F32),
            pltpu.VMEM((NF, CY, W0), F32),
            pltpu.VMEM((NF, CY, W0), F32),
            pltpu.VMEM((NF - 2, CY, W0), F32),
            pltpu.VMEM((8 * CY, W0), F32),
            pltpu.VMEM((8, Y1, LANES), F32),
            pltpu.VMEM((8, Y1, LANES), F32),
        ],
        compiler_params=PAR,
        name="before",
    )(place, f, u_lo, start, u_hi, from_left, from_right)


NX2, NZ2 = NDOM * X2, NGRP * Z2
NX3, NY3, NZ3 = NX2 // 2, Y2 // 2, NZ2 // 2
PAD2 = 4


def tables():
    def sine(n):
        k = np.arange(n) + 1.0
        t = np.sqrt(2.0 / (n + 1)) * np.sin(np.pi * np.outer(k, k) / (n + 1))
        return t, 2.0 - 2.0 * np.cos(np.pi * k / (n + 1))

    def cyclic(n):
        j = np.arange(n)[:, None]
        col = np.arange(n)[None, :]
        freq = (col + 1) // 2
        angle = 2.0 * np.pi * freq * j / n
        use_sine = (col % 2 == 0) & (col > 0)
        edge = (col == 0) | (col == n - 1)
        t = np.where(edge, np.sqrt(1.0 / n), np.sqrt(2.0 / n)) * np.where(
            use_sine, np.sin(angle), np.cos(angle)
        )
        return t, 2.0 - 2.0 * np.cos(2.0 * np.pi * freq[0] / n)

    tx, lx = sine(NX3)
    ty, ly = cyclic(NY3)
    tz, lz = sine(NZ3)
    txy = np.kron(tx, ty)
    lxy = (lx[:, None] + ly[None, :]).reshape(-1)
    scale = 64.0 / (lxy[:, None] + lz[None, :])
    return tuple(np.asarray(a, np.float32) for a in (txy, np.ascontiguousarray(txy.T), tz, scale))


def after_kernel(
    place, got, txy, txy_t, tz, scale, f1_own, f1_lo, f1_hi, u2, f,
    potential, totals, g, w, r, f3, e, e2, a1, b1, f1, ext, s1,
):
    dom, grp = place[0], place[1]
    zero2 = jnp.zeros((Y2, NZ2), F32)
    for p in range(PAD2):
        g[p] = zero2
        g[PAD2 + NX2 + p] = zero2
        w[p] = zero2
        w[PAD2 + NX2 + p] = zero2
        r[p] = zero2
        r[PAD2 + NX2 + p] = zero2
    slot = lanes_of((8, LANES)) // 32

    def gather(d, c):
        for i in range(2):
            for yb in range(2):
                s = 2 * i + yb
                for t in range(2):
                    row = None
                    for q in range(4):
                        piece = got[d * NGRP + 4 * t + q]
                        shift = (32 * (q - s)) % 128
                        piece = pltpu.roll(piece, shift, 1) if shift else piece
                        row = piece if row is None else jnp.where(slot == q, piece, row)
                    g[PAD2 + 2 * d + i, yb * 8 : yb * 8 + 8, t * LANES : (t + 1) * LANES] = row
        return c

    lax.fori_loop(0, NDOM, gather, 0, unroll=4)
    lane2 = lanes_of((1, NZ2))
    not_first = (lane2 > 0).astype(F32)
    not_last = (lane2 < NZ2 - 1).astype(F32)

    def beside2(ref, p):
        c = ref[p]
        around = (
            ref[p + 1]
            + ref[p - 1]
            + (pltpu.roll(c, 1, 0) + pltpu.roll(c, Y2 - 1, 0))
            + (pltpu.roll(c, 1, 1) * not_first + pltpu.roll(c, NZ2 - 1, 1) * not_last)
        )
        return c, around

    def start2(p, c):
        w[PAD2 + p] = g[PAD2 + p] * (16.0 / 9.0)
        return c

    lax.fori_loop(0, NX2, start2, 0, unroll=8)

    def sweep2(p, c):
        centre, around = beside2(w, PAD2 + p)
        r[PAD2 + p] = (3.0 * centre + around + 16.0 * g[PAD2 + p]) * (1.0 / 9.0)
        return c

    lax.fori_loop(0, NX2, sweep2, 0, unroll=8)

    def residue2(q, c):
        total = None
        for i in range(2):
            p = PAD2 + 2 * q + i
            centre, around = beside2(r, p)
            res = g[p] - (6.0 * centre - around) * (1.0 / 16.0)
            total = res if total is None else total + res
        f3[pl.ds(pl.multiple_of(q * Y2, Y2), Y2), :] = total
        return c

    lax.fori_loop(0, NX3, residue2, 0, unroll=4)
    z_sums = dot_right(f3[...], lane_halves(NZ3))
    n3 = NX3 * NY3
    ri = lax.broadcasted_iota(I32, (n3, 2 * n3), 0)
    ci = lax.broadcasted_iota(I32, (n3, 2 * n3), 1)
    source = dot_left(((ci // 2) == ri).astype(F32) * 0.125, z_sums)
    modes = dot(dot(txy_t[...], source), tz[...]) * scale[...]
    solved = dot(txy[...], dot(modes, tz[...]))
    rr = lax.broadcasted_iota(I32, (NZ3, NZ2), 0)
    cc = lax.broadcasted_iota(I32, (NZ3, NZ2), 1)
    wide = dot_right(solved, ((cc // 2) == rr).astype(F32))
    tall = dot_left(((lax.broadcasted_iota(I32, (2 * n3, n3), 0) // 2) == lax.broadcasted_iota(I32, (2 * n3, n3), 1)).astype(F32), wide)
    f3[...] = tall

    def add_coarse(q, c):
        for i in range(2):
            p = PAD2 + 2 * q + i
            r[p] = r[p] + f3[pl.ds(pl.multiple_of(q * Y2, Y2), Y2), :]
        return c

    lax.fori_loop(0, NX3, add_coarse, 0, unroll=4)
    first2 = 2 * dom

    def post2(src, dst, n, skip):
        for p in range(n):
            q = first2 + skip + p
            centre, around = beside2(src, q)
            new = (3.0 * centre + around + 16.0 * g[q]) * (1.0 / 9.0)
            dst[q] = new * x_ok(q - PAD2, NX2)

    post2(r, w, 8, 1)
    post2(w, r, 6, 2)
    lane = lanes_of((NZ2, LANES))
    signed = jnp.where(lane < 96, lane, lane - LANES)
    place_z = ((grp * Z1 + signed + 2 * NZ2) // 2 - NZ2 == rows_of((NZ2, LANES))).astype(F32)
    double_y = doubles(Y2)
    f1[0:3] = f1_lo[...]
    f1[3:11] = f1_own[...]
    f1[11:14] = f1_hi[...]
    mask1 = z_mask(LANES, Z1, grp, NGRP * Z1)

    def ok1(p):
        return mask1 * x_ok(dom * X1 + p - 5, NDOM * X1)

    for p in range(14):
        b1[p] = f1[p] * (4.0 / 9.0)
    fine = []
    for p in range(6):
        level2 = dot_right(r[first2 + 2 + p], place_z)
        fine.append(dot_left(double_y, level2))
    for p in range(1, 13):
        centre, around = beside(b1, p)
        new = (3.0 * centre + around + 4.0 * f1[p]) * (1.0 / 9.0)
        a1[p] = new * ok1(p) + fine[(p - 1) // 2] * mask1
    for p in range(2, 12):
        centre, around = beside(a1, p)
        b1[p] = (3.0 * centre + around + 4.0 * f1[p]) * (1.0 / 9.0) * ok1(p)
    for p in range(3, 11):
        centre, around = beside(b1, p)
        s1[(p - 3) * Y1 : (p - 2) * Y1, :] = (
            (3.0 * centre + around + 4.0 * f1[p]) * (1.0 / 9.0) * ok1(p)
        )
    r0 = lax.broadcasted_iota(I32, (LANES, W0), 0)
    c0 = lax.broadcasted_iota(I32, (LANES, W0), 1)
    spread0 = dot_right(s1[...], ((c0 // 2) == r0).astype(F32))
    double_y0 = doubles(Y1)
    for q in range(8):
        ext[q] = dot_left(double_y0, spread0[q * Y1 : (q + 1) * Y1, :])
    mask = z_mask(W0, CZ, grp, NGRP * CZ)

    def add_fine(p, c):
        e[p] = u2[p] + ext[(p + 1) // 2] * mask
        return c

    lax.fori_loop(0, 14, add_fine, 0, unroll=2)

    def last1(p, c):
        centre, around = beside(e, p + 1)
        new = (3.0 * centre + around + f[p]) * (1.0 / 9.0)
        e2[p] = new * (mask * x_ok(dom * CX + p - 2, NDOM * CX))
        return c

    lax.fori_loop(0, 12, last1, 0, unroll=4)

    def last2(p, c):
        centre, around = beside(e2, p + 1)
        new = (3.0 * centre + around + f[p + 1]) * (1.0 / 9.0)
        e[p] = new * (mask * x_ok(dom * CX + p - 1, NDOM * CX))
        return c

    lax.fori_loop(0, 10, last2, 0, unroll=5)

    def sums(x, carry):
        p = x + 1
        c = e[p]
        own = c[:, 0:LANES]
        potential[x] = own
        gx = 0.5 * (e[p + 1, :, 0:LANES] - e[p - 1, :, 0:LANES])
        gy = 0.5 * (pltpu.roll(own, CY - 1, 0) - pltpu.roll(own, 1, 0))
        gz = 0.5 * (pltpu.roll(c, W0 - 1, 1) - pltpu.roll(c, 1, 1))[:, 0:LANES]
        density = f[x + 2, :, 0:LANES]
        new = (gx * gx, gy * gy, gz * gz, gy * gz, gx * gz, gx * gy, own * density)
        return tuple(
            s + jnp.sum(v.reshape(8, 8, LANES), axis=0) for s, v in zip(carry, new)
        )

    zero = jnp.zeros((8, LANES), F32)
    parts = lax.fori_loop(0, CX, sums, (zero,) * 7, unroll=2)
    lane8 = lanes_of((1, LANES))
    line = jnp.zeros((1, LANES), F32)
    for i, part in enumerate(parts):
        line = jnp.where(lane8 == i, jnp.sum(part), line)
    totals[...] = jnp.broadcast_to(line, (NDEV, LANES))


def after(place, got, f1_own, f1_lo, f1_hi, u2, f):
    consts = [jnp.asarray(t) for t in tables()]
    return pl.pallas_call(
        after_kernel,
        out_shape=(sds(CX, CY, CZ), sds(NDEV, LANES)),
        in_specs=[SM] + [VM] * 10,
        out_specs=(VM, VM),
        scratch_shapes=[
            pltpu.VMEM((NX2 + 2 * PAD2, Y2, NZ2), F32),
            pltpu.VMEM((NX2 + 2 * PAD2, Y2, NZ2), F32),
            pltpu.VMEM((NX2 + 2 * PAD2, Y2, NZ2), F32),
            pltpu.VMEM((NX3 * Y2, NZ2), F32),
            pltpu.VMEM((14, CY, W0), F32),
            pltpu.VMEM((12, CY, W0), F32),
            pltpu.VMEM((14, Y1, LANES), F32),
            pltpu.VMEM((14, Y1, LANES), F32),
            pltpu.VMEM((14, Y1, LANES), F32),
            pltpu.VMEM((8, CY, W0), F32),
            pltpu.VMEM((8 * Y1, LANES), F32),
        ],
        input_output_aliases={},
        compiler_params=PAR,
        name="after",
    )(place, got, *consts, f1_own, f1_lo, f1_hi, u2, f)


def stress_kernel(got, out):
    total = jnp.sum(got[...], axis=0, keepdims=True)
    lane = lanes_of((1, LANES))
    energy = jnp.sum(jnp.where(lane == 6, total, 0.0))
    cells = float(NDOM * CX * CY * NGRP * CZ)
    line = total / cells - jnp.where(lane < 3, 0.5 * energy / cells, 0.0)
    out[...] = line[0, :6]


def stress_of(got):
    return pl.pallas_call(
        stress_kernel,
        out_shape=sds(6),
        in_specs=[VM],
        out_specs=VM,
        name="stress",
    )(got)


def shift(value, axis, distance):
    n = lax.axis_size(axis)
    route = [(i, i + distance) for i in range(n) if 0 <= i + distance < n]
    return lax.ppermute(value, axis, route)


def step(valence, start, tiles, home, ox, oy, oz, size):
    place = jnp.stack([lax.axis_index(DOM), lax.axis_index(GRP)]).astype(I32)
    lower = shift(start[CX - HU :], DOM, 1)
    upper = shift(start[:HU], DOM, -1)
    message = pack_atoms([v.reshape(-1) for v in (home, ox, oy, oz, size)], tiles)
    got = lax.all_to_all(message.reshape(NDEV, ROWS * LANES), ALL, 0, 0, tiled=True)
    got = got.reshape(NDEV * ROWS, LANES)
    u_left, u_right = edges(start, lower, upper)
    grid, up2, down = deposit(got, valence)
    from1 = shift(grid[2 * CY : 15 * CY].reshape(13, CY, LANES), DOM, 1)
    from2 = shift(up2.reshape(5, CY, LANES), DOM, 2)
    above = shift(down.reshape(6, CY, LANES), DOM, -1)
    f, left, right = join(
        grid, from1, from2, above, u_left, u_right
    )
    from_right = shift(left, GRP, -1)
    from_left = shift(right, GRP, 1)
    u2, fe, f1, chunk = before(place, f, lower, start, upper, from_left, from_right)
    f1_lo = shift(f1[1:4], DOM, 1)
    f1_hi = shift(f1[4:7], DOM, -1)
    everything = lax.all_to_all(chunk, ALL, 0, 0, tiled=True)
    potential, totals = after(place, everything, f1, f1_lo, f1_hi, u2, fe)
    sums = lax.all_to_all(totals, ALL, 0, 0, tiled=True)
    return potential, stress_of(sums)


def solution(mesh):
    split = Mesh(mesh.devices.reshape(4, 4, 4, 2), ("dom_0", "dom_1", "grp_0", "grp_1"))
    atoms = P(DOM + GRP, None)
    return jax.shard_map(
        step,
        mesh=split,
        in_specs=(P(DOM, None, GRP), P(DOM, None, GRP)) + (atoms,) * 6,
        out_specs=(P(DOM, None, GRP), P()),
        check_vma=False,
    )
```

```python
import functools

import jax
import jax.numpy as jnp
import numpy as np
from jax import lax
from jax.experimental import pallas as pl
from jax.experimental.pallas import tpu as pltpu
from jax.sharding import Mesh
from jax.sharding import PartitionSpec as P


CAP = 4
DOM = ("dom_0", "dom_1")
GRP = ("grp_0", "grp_1")
ALL = DOM + GRP
F32 = jnp.float32
I32 = jnp.int32
VM = pl.BlockSpec(memory_space=pltpu.VMEM)
SM = pl.BlockSpec(memory_space=pltpu.SMEM)

CX, CY, CZ = 8, 64, 128
NDOM, NGRP = 16, 8
NDEV = NDOM * NGRP
ATOMS = 256
TILE_ROWS = 4
LANES = 128
PAR = pltpu.CompilerParams(vmem_limit_bytes=16 * 1024 * 1024)


def sds(*shape, dtype=F32):
    return jax.ShapeDtypeStruct(shape, dtype)


def lanes_of(shape):
    return lax.broadcasted_iota(I32, shape, len(shape) - 1)


def rows_of(shape):
    return lax.broadcasted_iota(I32, shape, len(shape) - 2)


def split(a):
    hi = a.astype(jnp.bfloat16)
    return hi, (a - hi.astype(F32)).astype(jnp.bfloat16)


def dot3(a, b):
    (ah, al), (bh, bl) = split(a), split(b)
    low = jnp.dot(ah, bl, preferred_element_type=F32) + jnp.dot(al, bh, preferred_element_type=F32)
    return jnp.dot(ah, bh, preferred_element_type=F32) + low


def dot_right(a, ones):
    hi = a.astype(jnp.bfloat16)
    lo = (a - hi.astype(F32)).astype(jnp.bfloat16)
    ones = ones.astype(jnp.bfloat16)
    return jnp.dot(hi, ones, preferred_element_type=F32) + jnp.dot(
        lo, ones, preferred_element_type=F32
    )


def dot_left(ones, a):
    hi = a.astype(jnp.bfloat16)
    lo = (a - hi.astype(F32)).astype(jnp.bfloat16)
    ones = ones.astype(jnp.bfloat16)
    return jnp.dot(ones, hi, preferred_element_type=F32) + jnp.dot(
        ones, lo, preferred_element_type=F32
    )


ROWS = CAP * TILE_ROWS + 1


def pack_kernel(
    home_h, ox_h, oy_h, oz_h, size_h, tiles_h, out, rows, count, home, ox, oy, oz, size, tiles, sem
):
    copies = [
        pltpu.make_async_copy(src, dst, sem.at[i])
        for i, (src, dst) in enumerate(
            ((home_h, home), (ox_h, ox), (oy_h, oy), (oz_h, oz), (size_h, size), (tiles_h, tiles))
        )
    ]
    for copy in copies:
        copy.start()

    def clear_out(i, c):
        out[pl.ds(pl.multiple_of(i * 8, 8), 8), :] = jnp.zeros((8, LANES), F32)
        return c

    lax.fori_loop(0, NDEV * ROWS // 8, clear_out, 0, unroll=8)

    def clear(i, c):
        count[i] = 0
        return c

    lax.fori_loop(0, NDEV, clear, 0, unroll=8)
    copies[5].wait()
    lower = lanes_of((8, LANES)) < 64
    for g in range(ATOMS // 8):
        old = [tiles[g * 8 : g * 8 + 8, r * LANES : (r + 1) * LANES] for r in range(4)]
        turned = [pltpu.roll(v, 64, 1) for v in old]
        new = (
            jnp.where(lower, old[0], turned[2]),
            jnp.where(lower, turned[0], old[2]),
            jnp.where(lower, old[1], turned[3]),
            jnp.where(lower, turned[1], old[3]),
        )
        for r in range(TILE_ROWS):
            rows[pl.ds(g * 8 * TILE_ROWS + r, 8, stride=TILE_ROWS), :] = new[r]

    for copy in copies[:5]:
        copy.wait()
    lane = lanes_of((TILE_ROWS, LANES))
    need = rows_of((TILE_ROWS, LANES)) + jnp.where(lane < 64, 0, 4)
    need = jnp.maximum(jnp.maximum(need, (lane // 8) % 8), lane % 8)
    tile_c = lane % 8
    part1, slot1 = lanes_of((1, LANES)) & 3, lanes_of((1, LANES)) >> 2

    for start in range(0, ATOMS, PER_STEP):
        placed = []
        for n in range(start, start + PER_STEP):
            z_in = oz[n] & 7
            shift_ = (oy[n] & 15) * 8 + z_in
            value = rows[n * TILE_ROWS : (n + 1) * TILE_ROWS, :]
            value = jnp.where(need < size[n], value, 0.0)
            near = pltpu.roll(value, shift_, 1)
            far = pltpu.roll(value, shift_ + 120, 1)
            placed.append(jnp.where(tile_c >= z_in, near, far))
        for n in range(start, start + PER_STEP):
            to = home[n]
            rank = count[to]
            count[to] = rank + 1
            base = to * ROWS
            out[pl.ds(base + rank * TILE_ROWS, TILE_ROWS), :] = placed[n - start]
            line = jnp.where(part1 == 0, ox[n], jnp.where(part1 == 1, oy[n], oz[n]))
            pltpu.store(
                out.at[pl.ds(base + ROWS - 1, 1), :], line.astype(F32), mask=slot1 == rank
            )


PER_STEP = 16


def pack_atoms(scalars, tiles):
    return pl.pallas_call(
        pack_kernel,
        out_shape=sds(NDEV * ROWS, LANES),
        in_specs=[pl.BlockSpec(memory_space=pl.ANY)] * 6,
        out_specs=VM,
        scratch_shapes=[
            pltpu.VMEM((ATOMS * TILE_ROWS, LANES), F32),
            pltpu.SMEM((NDEV,), I32),
        ]
        + [pltpu.SMEM((ATOMS,), I32)] * 5
        + [pltpu.VMEM((ATOMS, TILE_ROWS * LANES), F32), pltpu.SemaphoreType.DMA((6,))],
        name="pack_atoms",
    )(*scalars, tiles)


ZB = CZ // 8 + 1
YB = 4


def deposit_kernel(got, valence, grid, up2, down, acc_a, acc_b, other, corner_v, corner_s, sem):
    part = lanes_of((8, LANES)) & 3
    for g in range(NDEV // 8):
        raw = got[pl.ds(g * 8 * ROWS + ROWS - 1, 8, stride=ROWS), :].astype(I32)
        back, ahead, ahead2 = (pltpu.roll(raw, n, 1) for n in (1, 127, 126))
        x = jnp.where(part == 0, raw, back)
        y = jnp.where(part == 0, ahead, jnp.where(part == 1, raw, back))
        z = jnp.where(part == 0, ahead2, jnp.where(part == 1, ahead, back))
        y_block = jnp.where(part == 1, ((y >> 4) + 1) & 3, y >> 4)
        row = (y_block * ZB + (z >> 3)) * 16 + x
        corner_v[g * 8 : g * 8 + 8, :] = jnp.where(
            part < 2, row, jnp.where(part == 2, (y & 15) * 8, z & 7)
        )
    copy = pltpu.make_async_copy(corner_v, corner_s, sem)
    copy.start()

    def turn(i, c):
        at = pl.ds(pl.multiple_of(i * 32, 8), 32)
        other[at, :] = pltpu.roll(got[at, :], 64, 1)
        return c

    lax.fori_loop(0, NDEV * ROWS // 32, turn, 0, unroll=4)

    def clear(i, c):
        zero = jnp.zeros((16, LANES), F32)
        acc_a[pl.ds(pl.multiple_of(i * 16, 16), 16), :] = zero
        acc_b[pl.ds(pl.multiple_of(i * 16, 16), 16), :] = zero
        return c

    lax.fori_loop(0, YB * ZB, clear, 0, unroll=4)
    copy.wait()
    lane = lanes_of((8, LANES))
    z_of = lane % 8

    for src in range(NDEV):
        for k in range(CAP):
            acc = acc_a if k % 2 == 0 else acc_b
            row = corner_s[src, 4 * k]
            wrapped = corner_s[src, 4 * k + 1]
            first = corner_s[src, 4 * k + 2]
            z_in = corner_s[src, 4 * k + 3]
            at = pl.ds(src * ROWS + k * TILE_ROWS, TILE_ROWS)
            value = jnp.concatenate([got[at, :], other[at, :]], axis=0)
            same = (lane >= first) & (lane < first + 64)
            here = jnp.where(same, value, 0.0)
            round_ = jnp.where(lane < first - 64, value, 0.0)
            near = z_of >= z_in
            a0 = acc[pl.ds(row, 8), :]
            a1 = acc[pl.ds(row + 16, 8), :]
            a2 = acc[pl.ds(wrapped, 8), :]
            a3 = acc[pl.ds(wrapped + 16, 8), :]
            acc[pl.ds(row, 8), :] = a0 + jnp.where(near, here, 0.0)
            acc[pl.ds(row + 16, 8), :] = a1 + jnp.where(near, 0.0, here)
            acc[pl.ds(wrapped, 8), :] = a2 + jnp.where(near, round_, 0.0)
            acc[pl.ds(wrapped + 16, 8), :] = a3 + jnp.where(near, 0.0, round_)
    group = lane // 8

    def lay_out(yb, c):
        for xg in range(2):
            blocks = []
            for zb in range(CZ // 8):
                at = pl.ds(pl.multiple_of((yb * ZB + zb) * 16 + xg * 8, 8), 8)
                blocks.append(acc_a[at, :] + acc_b[at, :])
            for s in (8, 4, 2, 1):
                low = (group & s) == 0
                for i in range(16):
                    if i & s == 0:
                        one_, two = blocks[i], blocks[i + s]
                        blocks[i] = jnp.where(low, one_, pltpu.roll(two, 8 * s, 1))
                        blocks[i + s] = jnp.where(low, pltpu.roll(one_, 128 - 8 * s, 1), two)
            for yy in range(16):
                grid[pl.ds(xg * 8 * CY + yb * 16 + yy, 8, stride=CY), :] = blocks[yy]
        return c

    lax.fori_loop(0, YB, lay_out, 0)
    grid[0 : CX * CY, :] += valence[...]
    up2[...] = grid[10 * CY : 15 * CY, :]
    down[...] = grid[0 : 6 * CY, :]


def deposit(got, valence):
    return pl.pallas_call(
        deposit_kernel,
        out_shape=(sds(16 * CY, LANES), sds(5 * CY, LANES), sds(6 * CY, LANES)),
        in_specs=[VM, VM],
        out_specs=(VM, VM, VM),
        scratch_shapes=[
            pltpu.VMEM((YB * ZB * 16, LANES), F32),
            pltpu.VMEM((YB * ZB * 16, LANES), F32),
            pltpu.VMEM((NDEV * ROWS, LANES), F32),
            pltpu.VMEM((NDEV, LANES), I32),
            pltpu.SMEM((NDEV, LANES), I32),
            pltpu.SemaphoreType.DMA,
        ],
        compiler_params=PAR,
        name="deposit",
    )(got, valence.reshape(CX * CY, LANES))


HU, HF = 7, 6
NU_, NF = CX + 2 * HU, CX + 2 * HF
UGROUPS, FGROUPS = -(-NU_ // 8), -(-NF // 8)
ZGROUPS = UGROUPS + FGROUPS


def u_plane(p, u_lo, start, u_hi):
    if p < HU:
        return u_lo[p]
    return start[p - HU] if p < HU + CX else u_hi[p - HU - CX]


def pack_edges(planes, left, right, at):
    slot = lanes_of((CY, LANES)) // 16
    for g in range(-(-len(planes) // 8)):
        lo = jnp.zeros((CY, LANES), F32)
        hi = jnp.zeros((CY, LANES), F32)
        for k, plane in enumerate(planes[g * 8 : g * 8 + 8]):
            plane = plane()
            plane = pltpu.roll(plane, 16 * k, 1) if k else plane
            lo = jnp.where(slot == k, plane, lo)
            hi = jnp.where(slot == (k - 1) % 8, plane, hi)
        left[at + g] = lo
        right[at + g] = hi


def edges_kernel(start, u_lo, u_hi, left, right):
    pack_edges(
        [functools.partial(u_plane, p, u_lo, start, u_hi) for p in range(NU_)], left, right, 0
    )


def edges(start, u_lo, u_hi):
    return pl.pallas_call(
        edges_kernel,
        out_shape=(sds(UGROUPS, CY, LANES),) * 2,
        in_specs=[VM] * 3,
        out_specs=(VM,) * 2,
        compiler_params=PAR,
        name="edges",
    )(start, u_lo, u_hi)


def join_kernel(grid, from1, from2, above, u_left, u_right, f, left, right):
    left[0:UGROUPS] = u_left[...]
    right[0:UGROUPS] = u_right[...]
    for p in range(NF):
        x = p - HF
        if x < 0:
            total = from1[x + 6]
            if x < -1:
                total = total + from2[x + 6]
        elif x < CX:
            total = grid[x * CY : (x + 1) * CY, :]
            if x < 7:
                total = total + from1[x + 6]
        else:
            total = above[x - CX]
            if x < 15:
                total = total + grid[x * CY : (x + 1) * CY, :]
        f[p] = total
    pack_edges([functools.partial(lambda q: f[q], p) for p in range(NF)], left, right, UGROUPS)


def join(*args):
    return pl.pallas_call(
        join_kernel,
        out_shape=(
            sds(NF, CY, LANES),
            sds(ZGROUPS, CY, LANES),
            sds(ZGROUPS, CY, LANES),
        ),
        in_specs=[VM] * 6,
        out_specs=(VM,) * 3,
        compiler_params=PAR,
        name="join",
    )(*args)


W0 = 256
X1, Y1, Z1 = 4, 32, 64
X2, Y2, Z2 = 2, 16, 32


def beside(ref, p):
    c = ref[p]
    n, w = c.shape
    return c, (
        ref[p + 1]
        + ref[p - 1]
        + (pltpu.roll(c, 1, 0) + pltpu.roll(c, n - 1, 0))
        + (pltpu.roll(c, 1, 1) + pltpu.roll(c, w - 1, 1))
    )


def z_mask(width, own, grp, total):
    lane = lanes_of((1, width))
    split = own + (width - own) // 2
    z = grp * own + jnp.where(lane < split, lane, lane - width)
    return ((z >= 0) & (z < total)).astype(F32)


def x_ok(x, total):
    return jnp.where((x >= 0) & (x < total), 1.0, 0.0).astype(F32)


def halves(n):
    r = lax.broadcasted_iota(I32, (n, 2 * n), 0)
    c = lax.broadcasted_iota(I32, (n, 2 * n), 1)
    return ((c // 2) == r).astype(F32)


def doubles(n):
    r = lax.broadcasted_iota(I32, (2 * n, n), 0)
    c = lax.broadcasted_iota(I32, (2 * n, n), 1)
    return ((r // 2) == c).astype(F32)


def lane_halves(n):
    r = lax.broadcasted_iota(I32, (2 * n, n), 0)
    c = lax.broadcasted_iota(I32, (2 * n, n), 1)
    return ((r // 2) == c).astype(F32)


STEP = CY + 16


def half_at(p, h):
    return (p * 2 + h) * STEP


def whole(ref, p, h):
    return ref[pl.ds(pl.multiple_of(half_at(p, h) + 8, 8), CY), :]


def put(ref, p, h, value):
    base = half_at(p, h)
    ref[pl.ds(pl.multiple_of(base + 8, 8), CY), :] = value
    ref[pl.ds(pl.multiple_of(base, 8), 8), :] = value[CY - 8 :]
    ref[pl.ds(pl.multiple_of(base + 8 + CY, 8), 8), :] = value[:8]


def moved(ref, p, h, by):
    return ref[pl.ds(half_at(p, h) + 8 + by, CY), :]


def z_sides(own, edge):
    lane = lanes_of(own.shape)
    first, last = lane == 0, lane == LANES - 1
    own_up, edge_up = pltpu.roll(own, LANES - 1, 1), pltpu.roll(edge, LANES - 1, 1)
    own_down, edge_down = pltpu.roll(own, 1, 1), pltpu.roll(edge, 1, 1)
    return (
        (jnp.where(last, edge_up, own_up), jnp.where(first, edge_down, own_down)),
        (jnp.where(last, own_up, edge_up), jnp.where(first, own_down, edge_down)),
    )


def beside0(ref, p):
    centre = [whole(ref, p, h) for h in range(2)]
    sides = z_sides(*centre)
    around = [
        (whole(ref, p + 1, h) + whole(ref, p - 1, h))
        + (moved(ref, p, h, 1) + moved(ref, p, h, -1))
        + (sides[h][0] + sides[h][1])
        for h in range(2)
    ]
    return centre, around


def before_kernel(
    place, f_in, u_lo, start, u_hi, from_left, from_right, u_out, f_out, f1, chunk, u, ua, fe, u2, pairs, v1, r1
):
    dom, grp = place[0], place[1]
    slot = lanes_of((CY, LANES)) // 16
    for p in range(NU_ + NF):
        g, k = (p // 8, p % 8) if p < NU_ else (UGROUPS + (p - NU_) // 8, (p - NU_) % 8)
        edge = jnp.where(slot == k, from_right[g], 0.0)
        edge = jnp.where(slot == (k - 1) % 8, from_left[g], edge)
        edge = pltpu.roll(edge, (-16 * k) % 128, 1) if k else edge
        if p < NU_:
            put(u, p, 0, u_plane(p, u_lo, start, u_hi))
            put(u, p, 1, edge)
        else:
            fe[p - NU_] = edge
    f = (f_in, fe)
    mask = z_mask(W0, CZ, grp, NGRP * CZ) * (1.0 / 9.0)
    mask = (mask[:, :LANES], mask[:, LANES:])

    def sweep1(p, c):
        centre, around = beside0(u, p + 1)
        ok = x_ok(dom * CX + p - HF, NDOM * CX)
        for h in range(2):
            put(ua, p, h, (3.0 * centre[h] + around[h] + f[h][p]) * (mask[h] * ok))
        return c

    lax.fori_loop(0, NF, sweep1, 0, unroll=4)

    def sweep2(p, c):
        centre, around = beside0(ua, p + 1)
        ok = x_ok(dom * CX + p - 5, NDOM * CX)
        for h in range(2):
            put(u2, p, h, (3.0 * centre[h] + around[h] + f[h][p + 1]) * (mask[h] * ok))
        return c

    lax.fori_loop(0, NF - 2, sweep2, 0, unroll=3)

    for p in range(14):
        for h in range(2):
            u_out[p, h] = whole(u2, p + 2, h)
    for p in range(12):
        for h in range(2):
            f_out[p, h] = f[h][p + 4]

    def residue0(q, c):
        total = [None, None]
        for i in range(2):
            p = 2 * q + i + 1
            centre, around = beside0(u2, p)
            for h in range(2):
                r = f[h][p + 1] - (6.0 * centre[h] - around[h])
                total[h] = r if total[h] is None else total[h] + r
        for h in range(2):
            pairs[pl.ds(pl.multiple_of(q * CY, CY), CY), h * LANES : (h + 1) * LANES] = total[h]
        return c

    lax.fori_loop(0, 8, residue0, 0, unroll=2)
    summed = dot_right(pairs[...], lane_halves(LANES))
    half_y = halves(Y1) * 0.125
    mask1 = z_mask(LANES, Z1, grp, NGRP * Z1)
    for q in range(8):
        part = dot_left(half_y, summed[q * CY : (q + 1) * CY, :])
        f1[q] = part * (mask1 * x_ok(dom * X1 + q - 2, NDOM * X1))
    for q in range(8):
        v1[q] = f1[q] * (4.0 / 9.0)
    for q in range(1, 7):
        centre, around = beside(v1, q)
        new = (3.0 * centre + around + 4.0 * f1[q]) * (1.0 / 9.0)
        r1[q] = new * (mask1 * x_ok(dom * X1 + q - 2, NDOM * X1))
    half_y2 = halves(Y2) * 0.125
    lane_half = lane_halves(LANES // 2)
    rows = []
    for i in range(2):
        total = None
        for j in range(2):
            q = 2 + 2 * i + j
            centre, around = beside(r1, q)
            r = f1[q] - (6.0 * centre - around) * 0.25
            total = r if total is None else total + r
        rows.append(total)
    both = dot_right(jnp.concatenate(rows, axis=0), jnp.concatenate([lane_half, jnp.zeros_like(lane_half)], axis=1))
    packed = jnp.zeros((8, LANES), F32)
    slot = lanes_of((8, LANES)) // 32
    for i in range(2):
        part = dot_left(half_y2, both[i * Y1 : (i + 1) * Y1, :])
        for yb in range(2):
            s = 2 * i + yb
            piece = part[yb * 8 : yb * 8 + 8, :]
            piece = pltpu.roll(piece, 32 * s, 1) if s else piece
            packed = jnp.where(slot == s, piece, packed)

    packed = pltpu.roll(packed, (grp & 3) * 32, 1)
    chunk[...] = packed


def before(place, f, u_lo, start, u_hi, from_left, from_right):
    return pl.pallas_call(
        before_kernel,
        out_shape=(
            sds(14, 2, CY, LANES),
            sds(12, 2, CY, LANES),
            sds(8, Y1, LANES),
            sds(8, LANES),
        ),
        in_specs=[SM] + [VM] * 6,
        out_specs=(VM,) * 4,
        scratch_shapes=[
            pltpu.VMEM((NU_ * 2 * STEP, LANES), F32),
            pltpu.VMEM((NF * 2 * STEP, LANES), F32),
            pltpu.VMEM((NF, CY, LANES), F32),
            pltpu.VMEM(((NF - 2) * 2 * STEP, LANES), F32),
            pltpu.VMEM((8 * CY, W0), F32),
            pltpu.VMEM((8, Y1, LANES), F32),
            pltpu.VMEM((8, Y1, LANES), F32),
        ],
        compiler_params=PAR,
        name="before",
    )(place, f, u_lo, start, u_hi, from_left, from_right)


NX2, NZ2 = NDOM * X2, NGRP * Z2
NX3, NY3, NZ3 = NX2 // 2, Y2 // 2, NZ2 // 2
PAD2 = 4


def tables():
    def sine(n):
        k = np.arange(n) + 1.0
        t = np.sqrt(2.0 / (n + 1)) * np.sin(np.pi * np.outer(k, k) / (n + 1))
        return t, 2.0 - 2.0 * np.cos(np.pi * k / (n + 1))

    def cyclic(n):
        j = np.arange(n)[:, None]
        col = np.arange(n)[None, :]
        freq = (col + 1) // 2
        angle = 2.0 * np.pi * freq * j / n
        use_sine = (col % 2 == 0) & (col > 0)
        edge = (col == 0) | (col == n - 1)
        t = np.where(edge, np.sqrt(1.0 / n), np.sqrt(2.0 / n)) * np.where(
            use_sine, np.sin(angle), np.cos(angle)
        )
        return t, 2.0 - 2.0 * np.cos(2.0 * np.pi * freq[0] / n)

    tx, lx = sine(NX3)
    ty, ly = cyclic(NY3)
    tz, lz = sine(NZ3)
    txy = np.kron(tx, ty)
    lxy = (lx[:, None] + ly[None, :]).reshape(-1)
    scale = 64.0 / (lxy[:, None] + lz[None, :])
    return tuple(np.asarray(a, np.float32) for a in (txy, np.ascontiguousarray(txy.T), tz, scale))


def after_kernel(
    place, got, txy, txy_t, tz, scale, f1_own, f1_lo, f1_hi, u2, f,
    potential, totals, g, w, r, f3, e, e2, a1, b1, f1, ext, s1,
):
    dom, grp = place[0], place[1]
    zero2 = jnp.zeros((Y2, NZ2), F32)
    for p in range(PAD2):
        g[p] = zero2
        g[PAD2 + NX2 + p] = zero2
        w[p] = zero2
        w[PAD2 + NX2 + p] = zero2
        r[p] = zero2
        r[PAD2 + NX2 + p] = zero2
    slot = lanes_of((8, LANES)) // 32

    def gather(d, c):
        for i in range(2):
            for yb in range(2):
                s = 2 * i + yb
                for t in range(2):
                    row = None
                    for q in range(4):
                        piece = got[d * NGRP + 4 * t + q]
                        row = piece if row is None else jnp.where(slot == (s + q) % 4, piece, row)
                    row = pltpu.roll(row, (-32 * s) % 128, 1) if s else row
                    g[PAD2 + 2 * d + i, yb * 8 : yb * 8 + 8, t * LANES : (t + 1) * LANES] = row
        return c

    lax.fori_loop(0, NDOM, gather, 0, unroll=4)
    lane2 = lanes_of((1, NZ2))
    not_first = (lane2 > 0).astype(F32)
    not_last = (lane2 < NZ2 - 1).astype(F32)

    def beside2(ref, p):
        c = ref[p]
        around = (
            ref[p + 1]
            + ref[p - 1]
            + (pltpu.roll(c, 1, 0) + pltpu.roll(c, Y2 - 1, 0))
            + (pltpu.roll(c, 1, 1) * not_first + pltpu.roll(c, NZ2 - 1, 1) * not_last)
        )
        return c, around

    def start2(p, c):
        w[PAD2 + p] = g[PAD2 + p] * (16.0 / 9.0)
        return c

    lax.fori_loop(0, NX2, start2, 0, unroll=8)

    def sweep2(p, c):
        centre, around = beside2(w, PAD2 + p)
        r[PAD2 + p] = (3.0 * centre + around + 16.0 * g[PAD2 + p]) * (1.0 / 9.0)
        return c

    lax.fori_loop(0, NX2, sweep2, 0, unroll=8)

    def residue2(q, c):
        total = None
        for i in range(2):
            p = PAD2 + 2 * q + i
            centre, around = beside2(r, p)
            res = g[p] - (6.0 * centre - around) * (1.0 / 16.0)
            total = res if total is None else total + res
        f3[pl.ds(pl.multiple_of(q * Y2, Y2), Y2), :] = total
        return c

    lax.fori_loop(0, NX3, residue2, 0, unroll=4)
    z_sums = dot_right(f3[...], lane_halves(NZ3))
    n3 = NX3 * NY3
    ri = lax.broadcasted_iota(I32, (n3, 2 * n3), 0)
    ci = lax.broadcasted_iota(I32, (n3, 2 * n3), 1)
    source = dot_left(((ci // 2) == ri).astype(F32) * 0.125, z_sums)
    modes = dot3(dot3(txy_t[...], source), tz[...]) * scale[...]
    solved = dot3(txy[...], dot3(modes, tz[...]))
    rr = lax.broadcasted_iota(I32, (NZ3, NZ2), 0)
    cc = lax.broadcasted_iota(I32, (NZ3, NZ2), 1)
    wide = dot_right(solved, ((cc // 2) == rr).astype(F32))
    tall = dot_left(((lax.broadcasted_iota(I32, (2 * n3, n3), 0) // 2) == lax.broadcasted_iota(I32, (2 * n3, n3), 1)).astype(F32), wide)
    f3[...] = tall

    def add_coarse(q, c):
        for i in range(2):
            p = PAD2 + 2 * q + i
            r[p] = r[p] + f3[pl.ds(pl.multiple_of(q * Y2, Y2), Y2), :]
        return c

    lax.fori_loop(0, NX3, add_coarse, 0, unroll=4)
    first2 = 2 * dom

    def post2(src, dst, n, skip):
        for p in range(n):
            q = first2 + skip + p
            centre, around = beside2(src, q)
            new = (3.0 * centre + around + 16.0 * g[q]) * (1.0 / 9.0)
            dst[q] = new * x_ok(q - PAD2, NX2)

    post2(r, w, 8, 1)
    post2(w, r, 6, 2)
    lane = lanes_of((NZ2, LANES))
    signed = jnp.where(lane < 96, lane, lane - LANES)
    place_z = ((grp * Z1 + signed + 2 * NZ2) // 2 - NZ2 == rows_of((NZ2, LANES))).astype(F32)
    f1[0:3] = f1_lo[...]
    f1[3:11] = f1_own[...]
    f1[11:14] = f1_hi[...]
    mask1 = z_mask(LANES, Z1, grp, NGRP * Z1)

    def ok1(p):
        return mask1 * x_ok(dom * X1 + p - 5, NDOM * X1)

    for p in range(14):
        b1[p] = f1[p] * (4.0 / 9.0)
    level2 = dot_right(r[pl.ds(first2 + 2, 6)].reshape(6 * Y2, NZ2), place_z)
    tall2 = dot_left(doubles(6 * Y2), level2)
    fine = [tall2[p * Y1 : (p + 1) * Y1, :] for p in range(6)]
    for p in range(1, 13):
        centre, around = beside(b1, p)
        new = (3.0 * centre + around + 4.0 * f1[p]) * (1.0 / 9.0)
        a1[p] = new * ok1(p) + fine[(p - 1) // 2] * mask1
    for p in range(2, 12):
        centre, around = beside(a1, p)
        b1[p] = (3.0 * centre + around + 4.0 * f1[p]) * (1.0 / 9.0) * ok1(p)
    for p in range(3, 11):
        centre, around = beside(b1, p)
        s1[(p - 3) * Y1 : (p - 2) * Y1, :] = (
            (3.0 * centre + around + 4.0 * f1[p]) * (1.0 / 9.0) * ok1(p)
        )
    r0 = lax.broadcasted_iota(I32, (LANES, W0), 0)
    c0 = lax.broadcasted_iota(I32, (LANES, W0), 1)
    spread0 = dot_right(s1[...], ((c0 // 2) == r0).astype(F32))
    double_y0 = doubles(Y1)
    for q in range(8):
        ext[q] = dot_left(double_y0, spread0[q * Y1 : (q + 1) * Y1, :])
    mask = z_mask(W0, CZ, grp, NGRP * CZ)
    mask = (mask[:, :LANES], mask[:, LANES:])
    mask9 = [m * (1.0 / 9.0) for m in mask]

    def add_fine(p, c):
        for h in range(2):
            fine0 = ext[(p + 1) // 2, :, h * LANES : (h + 1) * LANES]
            put(e, p, h, u2[p, h] + fine0 * mask[h])
        return c

    lax.fori_loop(0, 14, add_fine, 0, unroll=2)

    def last1(p, c):
        centre, around = beside0(e, p + 1)
        ok = x_ok(dom * CX + p - 2, NDOM * CX)
        for h in range(2):
            put(e2, p, h, (3.0 * centre[h] + around[h] + f[p, h]) * (mask9[h] * ok))
        return c

    lax.fori_loop(0, 12, last1, 0, unroll=4)

    def last2(p, c):
        centre, around = beside0(e2, p + 1)
        ok = x_ok(dom * CX + p - 1, NDOM * CX)
        for h in range(2):
            put(e, p, h, (3.0 * centre[h] + around[h] + f[p + 1, h]) * (mask9[h] * ok))
        return c

    lax.fori_loop(0, 10, last2, 0, unroll=5)

    def sums(x, carry):
        p = x + 1
        own = whole(e, p, 0)
        potential[x] = own
        gx = 0.5 * (whole(e, p + 1, 0) - whole(e, p - 1, 0))
        gy = 0.5 * (moved(e, p, 0, 1) - moved(e, p, 0, -1))
        (up, down), _ = z_sides(own, whole(e, p, 1))
        gz = 0.5 * (up - down)
        density = f[x + 2, 0]
        new = (gx * gx, gy * gy, gz * gz, gy * gz, gx * gz, gx * gy, own * density)
        return tuple(
            s + jnp.sum(v.reshape(8, 8, LANES), axis=0) for s, v in zip(carry, new)
        )

    zero = jnp.zeros((8, LANES), F32)
    parts = lax.fori_loop(0, CX, sums, (zero,) * 7, unroll=2)
    lane8 = lanes_of((1, LANES))
    line = jnp.zeros((1, LANES), F32)
    for i, part in enumerate(parts):
        line = jnp.where(lane8 == i, jnp.sum(part), line)
    totals[...] = jnp.broadcast_to(line, (NDEV, LANES))


def after(place, got, f1_own, f1_lo, f1_hi, u2, f):
    consts = [jnp.asarray(t) for t in tables()]
    return pl.pallas_call(
        after_kernel,
        out_shape=(sds(CX, CY, CZ), sds(NDEV, LANES)),
        in_specs=[SM] + [VM] * 10,
        out_specs=(VM, VM),
        scratch_shapes=[
            pltpu.VMEM((NX2 + 2 * PAD2, Y2, NZ2), F32),
            pltpu.VMEM((NX2 + 2 * PAD2, Y2, NZ2), F32),
            pltpu.VMEM((NX2 + 2 * PAD2, Y2, NZ2), F32),
            pltpu.VMEM((NX3 * Y2, NZ2), F32),
            pltpu.VMEM((14 * 2 * STEP, LANES), F32),
            pltpu.VMEM((12 * 2 * STEP, LANES), F32),
            pltpu.VMEM((14, Y1, LANES), F32),
            pltpu.VMEM((14, Y1, LANES), F32),
            pltpu.VMEM((14, Y1, LANES), F32),
            pltpu.VMEM((8, CY, W0), F32),
            pltpu.VMEM((8 * Y1, LANES), F32),
        ],
        input_output_aliases={},
        compiler_params=PAR,
        name="after",
    )(place, got, *consts, f1_own, f1_lo, f1_hi, u2, f)


def stress_kernel(got, out):
    total = jnp.sum(got[...], axis=0, keepdims=True)
    lane = lanes_of((1, LANES))
    energy = jnp.sum(jnp.where(lane == 6, total, 0.0))
    cells = float(NDOM * CX * CY * NGRP * CZ)
    line = total / cells - jnp.where(lane < 3, 0.5 * energy / cells, 0.0)
    out[...] = line[0, :6]


def stress_of(got):
    return pl.pallas_call(
        stress_kernel,
        out_shape=sds(6),
        in_specs=[VM],
        out_specs=VM,
        name="stress",
    )(got)


def shift(value, axis, distance):
    n = lax.axis_size(axis)
    route = [(i, i + distance) for i in range(n) if 0 <= i + distance < n]
    return lax.ppermute(value, axis, route)


def step(valence, start, tiles, home, ox, oy, oz, size):
    place = jnp.stack([lax.axis_index(DOM), lax.axis_index(GRP)]).astype(I32)
    lower = shift(start[CX - HU :], DOM, 1)
    upper = shift(start[:HU], DOM, -1)
    message = pack_atoms([v.reshape(-1) for v in (home, ox, oy, oz, size)], tiles)
    got = lax.all_to_all(message.reshape(NDEV, ROWS * LANES), ALL, 0, 0, tiled=True)
    got = got.reshape(NDEV * ROWS, LANES)
    u_left, u_right = edges(start, lower, upper)
    grid, up2, down = deposit(got, valence)
    from1 = shift(grid[2 * CY : 15 * CY].reshape(13, CY, LANES), DOM, 1)
    from2 = shift(up2.reshape(5, CY, LANES), DOM, 2)
    above = shift(down.reshape(6, CY, LANES), DOM, -1)
    f, left, right = join(
        grid, from1, from2, above, u_left, u_right
    )
    from_right = shift(left, GRP, -1)
    from_left = shift(right, GRP, 1)
    u2, fe, f1, chunk = before(place, f, lower, start, upper, from_left, from_right)
    f1_lo = shift(f1[1:4], DOM, 1)
    f1_hi = shift(f1[4:7], DOM, -1)
    chunks = jnp.broadcast_to(chunk[None], (NDEV, 8, LANES))
    everything = lax.all_to_all(chunks, ALL, 0, 0, tiled=True)
    potential, totals = after(place, everything, f1, f1_lo, f1_hi, u2, fe)
    sums = lax.all_to_all(totals, ALL, 0, 0, tiled=True)
    return potential, stress_of(sums)


def solution(mesh):
    split = Mesh(mesh.devices.reshape(4, 4, 4, 2), ("dom_0", "dom_1", "grp_0", "grp_1"))
    atoms = P(DOM + GRP, None)
    return jax.shard_map(
        step,
        mesh=split,
        in_specs=(P(DOM, None, GRP), P(DOM, None, GRP)) + (atoms,) * 6,
        out_specs=(P(DOM, None, GRP), P()),
        check_vma=False,
    )
```

```python
import functools

import jax
import jax.numpy as jnp
import numpy as np
from jax import lax
from jax.experimental import pallas as pl
from jax.experimental.pallas import tpu as pltpu
from jax.sharding import Mesh
from jax.sharding import PartitionSpec as P


CAP = 4
DOM = ("dom_0", "dom_1")
GRP = ("grp_0", "grp_1")
ALL = DOM + GRP
F32 = jnp.float32
I32 = jnp.int32
VM = pl.BlockSpec(memory_space=pltpu.VMEM)
SM = pl.BlockSpec(memory_space=pltpu.SMEM)

CX, CY, CZ = 8, 64, 128
NDOM, NGRP = 16, 8
NDEV = NDOM * NGRP
ATOMS = 256
TILE_ROWS = 4
LANES = 128
PAR = pltpu.CompilerParams(vmem_limit_bytes=16 * 1024 * 1024)


def sds(*shape, dtype=F32):
    return jax.ShapeDtypeStruct(shape, dtype)


def lanes_of(shape):
    return lax.broadcasted_iota(I32, shape, len(shape) - 1)


def rows_of(shape):
    return lax.broadcasted_iota(I32, shape, len(shape) - 2)


def split(a):
    hi = a.astype(jnp.bfloat16)
    return hi, (a - hi.astype(F32)).astype(jnp.bfloat16)


def dot3(a, b):
    (ah, al), (bh, bl) = split(a), split(b)
    low = jnp.dot(ah, bl, preferred_element_type=F32) + jnp.dot(al, bh, preferred_element_type=F32)
    return jnp.dot(ah, bh, preferred_element_type=F32) + low


def dot_right(a, ones):
    hi = a.astype(jnp.bfloat16)
    lo = (a - hi.astype(F32)).astype(jnp.bfloat16)
    ones = ones.astype(jnp.bfloat16)
    return jnp.dot(hi, ones, preferred_element_type=F32) + jnp.dot(
        lo, ones, preferred_element_type=F32
    )


def dot_left(ones, a):
    hi = a.astype(jnp.bfloat16)
    lo = (a - hi.astype(F32)).astype(jnp.bfloat16)
    ones = ones.astype(jnp.bfloat16)
    return jnp.dot(ones, hi, preferred_element_type=F32) + jnp.dot(
        ones, lo, preferred_element_type=F32
    )


ROWS = CAP * TILE_ROWS + 1


def pack_kernel(
    home_h, ox_h, oy_h, oz_h, size_h, tiles_h, out, rows, count, home, ox, oy, oz, size, tiles, sem
):
    copies = [
        pltpu.make_async_copy(src, dst, sem.at[i])
        for i, (src, dst) in enumerate(
            ((home_h, home), (ox_h, ox), (oy_h, oy), (oz_h, oz), (size_h, size), (tiles_h, tiles))
        )
    ]
    for copy in copies:
        copy.start()

    def clear_out(i, c):
        out[pl.ds(pl.multiple_of(i * 8, 8), 8), :] = jnp.zeros((8, LANES), F32)
        return c

    lax.fori_loop(0, NDEV * ROWS // 8, clear_out, 0, unroll=8)

    def clear(i, c):
        count[i] = 0
        return c

    lax.fori_loop(0, NDEV, clear, 0, unroll=8)
    copies[5].wait()
    lower = lanes_of((8, LANES)) < 64
    for g in range(ATOMS // 8):
        old = [tiles[g * 8 : g * 8 + 8, r * LANES : (r + 1) * LANES] for r in range(4)]
        turned = [pltpu.roll(v, 64, 1) for v in old]
        new = (
            jnp.where(lower, old[0], turned[2]),
            jnp.where(lower, turned[0], old[2]),
            jnp.where(lower, old[1], turned[3]),
            jnp.where(lower, turned[1], old[3]),
        )
        for r in range(TILE_ROWS):
            rows[pl.ds(g * 8 * TILE_ROWS + r, 8, stride=TILE_ROWS), :] = new[r]

    for copy in copies[:5]:
        copy.wait()
    lane = lanes_of((TILE_ROWS, LANES))
    need = rows_of((TILE_ROWS, LANES)) + jnp.where(lane < 64, 0, 4)
    need = jnp.maximum(jnp.maximum(need, (lane >> 3) & 7), lane & 7)
    tile_c = lane & 7
    part1, slot1 = lanes_of((1, LANES)) & 3, lanes_of((1, LANES)) >> 2

    for start in range(0, ATOMS, PER_STEP):
        placed = []
        for n in range(start, start + PER_STEP):
            z_in = oz[n] & 7
            shift_ = (oy[n] & 15) * 8 + z_in
            value = rows[n * TILE_ROWS : (n + 1) * TILE_ROWS, :]
            value = jnp.where(need < size[n], value, 0.0)
            near = pltpu.roll(value, shift_, 1)
            far = pltpu.roll(value, shift_ + 120, 1)
            placed.append(jnp.where(tile_c >= z_in, near, far))
        for n in range(start, start + PER_STEP):
            to = home[n]
            rank = count[to]
            count[to] = rank + 1
            base = to * ROWS
            out[pl.ds(base + rank * TILE_ROWS, TILE_ROWS), :] = placed[n - start]
            line = jnp.where(part1 == 0, ox[n], jnp.where(part1 == 1, oy[n], oz[n]))
            pltpu.store(
                out.at[pl.ds(base + ROWS - 1, 1), :], line.astype(F32), mask=slot1 == rank
            )


PER_STEP = 16


def pack_atoms(scalars, tiles):
    return pl.pallas_call(
        pack_kernel,
        out_shape=sds(NDEV * ROWS, LANES),
        in_specs=[pl.BlockSpec(memory_space=pl.ANY)] * 6,
        out_specs=VM,
        scratch_shapes=[
            pltpu.VMEM((ATOMS * TILE_ROWS, LANES), F32),
            pltpu.SMEM((NDEV,), I32),
        ]
        + [pltpu.SMEM((ATOMS,), I32)] * 5
        + [pltpu.VMEM((ATOMS, TILE_ROWS * LANES), F32), pltpu.SemaphoreType.DMA((6,))],
        name="pack_atoms",
    )(*scalars, tiles)


ZB = CZ // 8 + 1
YB = 4


def deposit_kernel(got, valence, grid, up2, down, acc_a, acc_b, other, corner_v, corner_s, sem):
    part = lanes_of((8, LANES)) & 3
    for g in range(NDEV // 8):
        raw = got[pl.ds(g * 8 * ROWS + ROWS - 1, 8, stride=ROWS), :].astype(I32)
        back, ahead, ahead2 = (pltpu.roll(raw, n, 1) for n in (1, 127, 126))
        x = jnp.where(part == 0, raw, back)
        y = jnp.where(part == 0, ahead, jnp.where(part == 1, raw, back))
        z = jnp.where(part == 0, ahead2, jnp.where(part == 1, ahead, back))
        y_block = jnp.where(part == 1, ((y >> 4) + 1) & 3, y >> 4)
        row = (y_block * ZB + (z >> 3)) * 16 + x
        corner_v[g * 8 : g * 8 + 8, :] = jnp.where(
            part < 2, row, jnp.where(part == 2, (y & 15) * 8, z & 7)
        )
    copy = pltpu.make_async_copy(corner_v, corner_s, sem)
    copy.start()

    def turn(i, c):
        at = pl.ds(pl.multiple_of(i * 32, 8), 32)
        other[at, :] = pltpu.roll(got[at, :], 64, 1)
        return c

    lax.fori_loop(0, NDEV * ROWS // 32, turn, 0, unroll=4)

    def clear(i, c):
        zero = jnp.zeros((16, LANES), F32)
        acc_a[pl.ds(pl.multiple_of(i * 16, 16), 16), :] = zero
        acc_b[pl.ds(pl.multiple_of(i * 16, 16), 16), :] = zero
        return c

    lax.fori_loop(0, YB * ZB, clear, 0, unroll=4)
    copy.wait()
    lane = lanes_of((8, LANES))
    z_of = lane & 7

    for src in range(NDEV):
        for k in range(CAP):
            acc = acc_a if k % 2 == 0 else acc_b
            row = corner_s[src, 4 * k]
            wrapped = corner_s[src, 4 * k + 1]
            first = corner_s[src, 4 * k + 2]
            z_in = corner_s[src, 4 * k + 3]
            at = pl.ds(src * ROWS + k * TILE_ROWS, TILE_ROWS)
            value = jnp.concatenate([got[at, :], other[at, :]], axis=0)
            same = (lane >= first) & (lane < first + 64)
            here = jnp.where(same, value, 0.0)
            round_ = jnp.where(lane < first - 64, value, 0.0)
            near = z_of >= z_in
            a0 = acc[pl.ds(row, 8), :]
            a1 = acc[pl.ds(row + 16, 8), :]
            a2 = acc[pl.ds(wrapped, 8), :]
            a3 = acc[pl.ds(wrapped + 16, 8), :]
            acc[pl.ds(row, 8), :] = a0 + jnp.where(near, here, 0.0)
            acc[pl.ds(row + 16, 8), :] = a1 + jnp.where(near, 0.0, here)
            acc[pl.ds(wrapped, 8), :] = a2 + jnp.where(near, round_, 0.0)
            acc[pl.ds(wrapped + 16, 8), :] = a3 + jnp.where(near, 0.0, round_)
    group = lane >> 3

    def lay_out(yb, c):
        for xg in range(2):
            blocks = []
            for zb in range(CZ // 8):
                at = pl.ds(pl.multiple_of((yb * ZB + zb) * 16 + xg * 8, 8), 8)
                blocks.append(acc_a[at, :] + acc_b[at, :])
            for s in (8, 4, 2, 1):
                low = (group & s) == 0
                for i in range(16):
                    if i & s == 0:
                        one_, two = blocks[i], blocks[i + s]
                        blocks[i] = jnp.where(low, one_, pltpu.roll(two, 8 * s, 1))
                        blocks[i + s] = jnp.where(low, pltpu.roll(one_, 128 - 8 * s, 1), two)
            for yy in range(16):
                grid[pl.ds(xg * 8 * CY + yb * 16 + yy, 8, stride=CY), :] = blocks[yy]
        return c

    lax.fori_loop(0, YB, lay_out, 0)
    grid[0 : CX * CY, :] += valence[...]
    up2[...] = grid[10 * CY : 15 * CY, :]
    down[...] = grid[0 : 6 * CY, :]


def deposit(got, valence):
    return pl.pallas_call(
        deposit_kernel,
        out_shape=(sds(16 * CY, LANES), sds(5 * CY, LANES), sds(6 * CY, LANES)),
        in_specs=[VM, VM],
        out_specs=(VM, VM, VM),
        scratch_shapes=[
            pltpu.VMEM((YB * ZB * 16, LANES), F32),
            pltpu.VMEM((YB * ZB * 16, LANES), F32),
            pltpu.VMEM((NDEV * ROWS, LANES), F32),
            pltpu.VMEM((NDEV, LANES), I32),
            pltpu.SMEM((NDEV, LANES), I32),
            pltpu.SemaphoreType.DMA,
        ],
        compiler_params=PAR,
        name="deposit",
    )(got, valence.reshape(CX * CY, LANES))


HU, HF = 7, 6
NU_, NF = CX + 2 * HU, CX + 2 * HF
UGROUPS, FGROUPS = -(-NU_ // 8), -(-NF // 8)


def u_plane(p, u_lo, start, u_hi):
    if p < HU:
        return u_lo[p]
    return start[p - HU] if p < HU + CX else u_hi[p - HU - CX]


def pack_edges(planes, left, right, at):
    slot = lanes_of((CY, LANES)) >> 4
    for g in range(-(-len(planes) // 8)):
        lo = jnp.zeros((CY, LANES), F32)
        hi = jnp.zeros((CY, LANES), F32)
        for k, plane in enumerate(planes[g * 8 : g * 8 + 8]):
            plane = plane()
            plane = pltpu.roll(plane, 16 * k, 1) if k else plane
            lo = jnp.where(slot == k, plane, lo)
            hi = jnp.where(slot == (k - 1) % 8, plane, hi)
        left[at + g] = lo
        right[at + g] = hi


def edges_kernel(start, u_lo, u_hi, left, right):
    pack_edges(
        [functools.partial(u_plane, p, u_lo, start, u_hi) for p in range(NU_)], left, right, 0
    )


def edges(start, u_lo, u_hi):
    return pl.pallas_call(
        edges_kernel,
        out_shape=(sds(UGROUPS, CY, LANES),) * 2,
        in_specs=[VM] * 3,
        out_specs=(VM,) * 2,
        compiler_params=PAR,
        name="edges",
    )(start, u_lo, u_hi)


def join_kernel(grid, from1, from2, above, f, left, right):
    for p in range(NF):
        x = p - HF
        if x < 0:
            total = from1[x + 6]
            if x < -1:
                total = total + from2[x + 6]
        elif x < CX:
            total = grid[x * CY : (x + 1) * CY, :]
            if x < 7:
                total = total + from1[x + 6]
        else:
            total = above[x - CX]
            if x < 15:
                total = total + grid[x * CY : (x + 1) * CY, :]
        f[p] = total
    pack_edges([functools.partial(lambda q: f[q], p) for p in range(NF)], left, right, 0)


def join(*args):
    return pl.pallas_call(
        join_kernel,
        out_shape=(
            sds(NF, CY, LANES),
            sds(FGROUPS, CY, LANES),
            sds(FGROUPS, CY, LANES),
        ),
        in_specs=[VM] * 4,
        out_specs=(VM,) * 3,
        compiler_params=PAR,
        name="join",
    )(*args)


W0 = 256
X1, Y1, Z1 = 4, 32, 64
X2, Y2, Z2 = 2, 16, 32


def beside(ref, p):
    c = ref[p]
    n, w = c.shape
    return c, (
        ref[p + 1]
        + ref[p - 1]
        + (pltpu.roll(c, 1, 0) + pltpu.roll(c, n - 1, 0))
        + (pltpu.roll(c, 1, 1) + pltpu.roll(c, w - 1, 1))
    )


def z_mask(width, own, grp, total):
    lane = lanes_of((1, width))
    split = own + (width - own) // 2
    z = grp * own + jnp.where(lane < split, lane, lane - width)
    return ((z >= 0) & (z < total)).astype(F32)


def x_ok(x, total):
    return jnp.where((x >= 0) & (x < total), 1.0, 0.0).astype(F32)


def halves(n):
    r = lax.broadcasted_iota(I32, (n, 2 * n), 0)
    c = lax.broadcasted_iota(I32, (n, 2 * n), 1)
    return ((c >> 1) == r).astype(F32)


def doubles(n):
    r = lax.broadcasted_iota(I32, (2 * n, n), 0)
    c = lax.broadcasted_iota(I32, (2 * n, n), 1)
    return ((r >> 1) == c).astype(F32)


def lane_halves(n):
    r = lax.broadcasted_iota(I32, (2 * n, n), 0)
    c = lax.broadcasted_iota(I32, (2 * n, n), 1)
    return ((r >> 1) == c).astype(F32)


STEP = CY + 16


def half_at(p, h):
    return (p * 2 + h) * STEP


PART = 32


def whole(ref, p, h, row=0, n=CY):
    return ref[pl.ds(pl.multiple_of(half_at(p, h) + 8 + row, 8), n), :]


def put(ref, p, h, value, row=0):
    base = half_at(p, h)
    n = value.shape[0]
    ref[pl.ds(pl.multiple_of(base + 8 + row, 8), n), :] = value
    if row + n == CY:
        ref[pl.ds(pl.multiple_of(base, 8), 8), :] = value[n - 8 :]
    if row == 0:
        ref[pl.ds(pl.multiple_of(base + 8 + CY, 8), 8), :] = value[:8]


def moved(ref, p, h, by, row=0, n=CY):
    return ref[pl.ds(half_at(p, h) + 8 + row + by, n), :]


def z_sides(own, edge):
    lane = lanes_of(own.shape)
    first, last = lane == 0, lane == LANES - 1
    own_up, edge_up = pltpu.roll(own, LANES - 1, 1), pltpu.roll(edge, LANES - 1, 1)
    own_down, edge_down = pltpu.roll(own, 1, 1), pltpu.roll(edge, 1, 1)
    return (
        (jnp.where(last, edge_up, own_up), jnp.where(first, edge_down, own_down)),
        (jnp.where(last, own_up, edge_up), jnp.where(first, own_down, edge_down)),
    )


def beside0(ref, p, row):
    centre = [whole(ref, p, h, row, PART) for h in range(2)]
    sides = z_sides(*centre)
    around = [
        (whole(ref, p + 1, h, row, PART) + whole(ref, p - 1, h, row, PART))
        + (moved(ref, p, h, 1, row, PART) + moved(ref, p, h, -1, row, PART))
        + (sides[h][0] + sides[h][1])
        for h in range(2)
    ]
    return centre, around


def sweep0(src, dst, f, p, shift_u, shift_f, mask, ok):
    for row in range(0, CY, PART):
        centre, around = beside0(src, p + shift_u, row)
        for h in range(2):
            new = 3.0 * centre[h] + around[h] + f(p + shift_f, h, row)
            put(dst, p, h, new * (mask[h] * ok), row)


def before_kernel(
    place, f_in, u_lo, start, u_hi, u_from_left, u_from_right, f_from_left, f_from_right, u_out, f_out, f1, chunk, u, ua, fe, u2, pairs, v1, r1
):
    dom, grp = place[0], place[1]
    slot = lanes_of((CY, LANES)) >> 4
    for p in range(NU_ + NF):
        if p < NU_:
            g, k, from_left, from_right = p // 8, p % 8, u_from_left, u_from_right
        else:
            g, k, from_left, from_right = (p - NU_) // 8, (p - NU_) % 8, f_from_left, f_from_right
        edge = jnp.where(slot == k, from_right[g], 0.0)
        edge = jnp.where(slot == (k - 1) % 8, from_left[g], edge)
        edge = pltpu.roll(edge, (-16 * k) % 128, 1) if k else edge
        if p < NU_:
            put(u, p, 0, u_plane(p, u_lo, start, u_hi))
            put(u, p, 1, edge)
        else:
            fe[p - NU_] = edge
    f = (f_in, fe)

    def source(p, h, row):
        return f[h][p, row : row + PART, :]

    mask = z_mask(W0, CZ, grp, NGRP * CZ) * (1.0 / 9.0)
    mask = (mask[:, :LANES], mask[:, LANES:])

    def sweep1(p, c):
        sweep0(u, ua, source, p, 1, 0, mask, x_ok(dom * CX + p - HF, NDOM * CX))
        return c

    lax.fori_loop(0, NF, sweep1, 0, unroll=4)

    def sweep2(p, c):
        sweep0(ua, u2, source, p, 1, 1, mask, x_ok(dom * CX + p - 5, NDOM * CX))
        return c

    lax.fori_loop(0, NF - 2, sweep2, 0, unroll=3)

    for p in range(14):
        for h in range(2):
            u_out[p, h] = whole(u2, p + 2, h)
    for p in range(12):
        for h in range(2):
            f_out[p, h] = f[h][p + 4]

    def residue0(q, c):
        for row in range(0, CY, PART):
            total = [None, None]
            for i in range(2):
                p = 2 * q + i + 1
                centre, around = beside0(u2, p, row)
                for h in range(2):
                    r = source(p + 1, h, row) - (6.0 * centre[h] - around[h])
                    total[h] = r if total[h] is None else total[h] + r
            at = pl.ds(pl.multiple_of(q * CY + row, 8), PART)
            for h in range(2):
                pairs[at, h * LANES : (h + 1) * LANES] = total[h]
        return c

    lax.fori_loop(0, 8, residue0, 0, unroll=2)
    summed = dot_right(pairs[...], lane_halves(LANES))
    half_y = halves(Y1) * 0.125
    mask1 = z_mask(LANES, Z1, grp, NGRP * Z1)
    for q in range(8):
        part = dot_left(half_y, summed[q * CY : (q + 1) * CY, :])
        f1[q] = part * (mask1 * x_ok(dom * X1 + q - 2, NDOM * X1))
    for q in range(8):
        v1[q] = f1[q] * (4.0 / 9.0)
    for q in range(1, 7):
        centre, around = beside(v1, q)
        new = centre * (4.0 / 3.0) + around * (1.0 / 9.0)
        r1[q] = new * (mask1 * x_ok(dom * X1 + q - 2, NDOM * X1))
    half_y2 = halves(Y2) * 0.125
    lane_half = lane_halves(LANES // 2)
    rows = []
    for i in range(2):
        total = None
        for j in range(2):
            q = 2 + 2 * i + j
            centre, around = beside(r1, q)
            r = f1[q] - (6.0 * centre - around) * 0.25
            total = r if total is None else total + r
        rows.append(total)
    both = dot_right(jnp.concatenate(rows, axis=0), jnp.concatenate([lane_half, jnp.zeros_like(lane_half)], axis=1))
    packed = jnp.zeros((8, LANES), F32)
    slot = lanes_of((8, LANES)) >> 5
    for i in range(2):
        part = dot_left(half_y2, both[i * Y1 : (i + 1) * Y1, :])
        for yb in range(2):
            s = 2 * i + yb
            piece = part[yb * 8 : yb * 8 + 8, :]
            piece = pltpu.roll(piece, 32 * s, 1) if s else piece
            packed = jnp.where(slot == s, piece, packed)

    packed = pltpu.roll(packed, (grp & 3) * 32, 1)
    chunk[...] = packed


def before(place, *args):
    return pl.pallas_call(
        before_kernel,
        out_shape=(
            sds(14, 2, CY, LANES),
            sds(12, 2, CY, LANES),
            sds(8, Y1, LANES),
            sds(8, LANES),
        ),
        in_specs=[SM] + [VM] * 8,
        out_specs=(VM,) * 4,
        scratch_shapes=[
            pltpu.VMEM((NU_ * 2 * STEP, LANES), F32),
            pltpu.VMEM((NF * 2 * STEP, LANES), F32),
            pltpu.VMEM((NF, CY, LANES), F32),
            pltpu.VMEM(((NF - 2) * 2 * STEP, LANES), F32),
            pltpu.VMEM((8 * CY, W0), F32),
            pltpu.VMEM((8, Y1, LANES), F32),
            pltpu.VMEM((8, Y1, LANES), F32),
        ],
        compiler_params=PAR,
        name="before",
    )(place, *args)


NX2, NZ2 = NDOM * X2, NGRP * Z2
NX3, NY3, NZ3 = NX2 // 2, Y2 // 2, NZ2 // 2
PAD2 = 4


def tables():
    def sine(n):
        k = np.arange(n) + 1.0
        t = np.sqrt(2.0 / (n + 1)) * np.sin(np.pi * np.outer(k, k) / (n + 1))
        return t, 2.0 - 2.0 * np.cos(np.pi * k / (n + 1))

    def cyclic(n):
        j = np.arange(n)[:, None]
        col = np.arange(n)[None, :]
        freq = (col + 1) // 2
        angle = 2.0 * np.pi * freq * j / n
        use_sine = (col % 2 == 0) & (col > 0)
        edge = (col == 0) | (col == n - 1)
        t = np.where(edge, np.sqrt(1.0 / n), np.sqrt(2.0 / n)) * np.where(
            use_sine, np.sin(angle), np.cos(angle)
        )
        return t, 2.0 - 2.0 * np.cos(2.0 * np.pi * freq[0] / n)

    tx, lx = sine(NX3)
    ty, ly = cyclic(NY3)
    tz, lz = sine(NZ3)
    txy = np.kron(tx, ty)
    lxy = (lx[:, None] + ly[None, :]).reshape(-1)
    scale = 64.0 / (lxy[:, None] + lz[None, :])
    return tuple(np.asarray(a, np.float32) for a in (txy, np.ascontiguousarray(txy.T), tz, scale))


def after_kernel(
    place, got, txy, txy_t, tz, scale, f1_own, f1_lo, f1_hi, u2, f,
    potential, totals, g, w, r, f3, e, e2, a1, b1, f1, ext, s1,
):
    dom, grp = place[0], place[1]
    zero2 = jnp.zeros((Y2, NZ2), F32)
    for p in range(PAD2):
        g[p] = zero2
        g[PAD2 + NX2 + p] = zero2
        w[p] = zero2
        w[PAD2 + NX2 + p] = zero2
        r[p] = zero2
        r[PAD2 + NX2 + p] = zero2
    slot = lanes_of((8, LANES)) >> 5

    def gather(d, c):
        for i in range(2):
            for yb in range(2):
                s = 2 * i + yb
                for t in range(2):
                    row = None
                    for q in range(4):
                        piece = got[d * NGRP + 4 * t + q]
                        row = piece if row is None else jnp.where(slot == (s + q) % 4, piece, row)
                    row = pltpu.roll(row, (-32 * s) % 128, 1) if s else row
                    g[PAD2 + 2 * d + i, yb * 8 : yb * 8 + 8, t * LANES : (t + 1) * LANES] = row
        return c

    lax.fori_loop(0, NDOM, gather, 0, unroll=4)
    lane2 = lanes_of((1, NZ2))
    not_first = (lane2 > 0).astype(F32)
    not_last = (lane2 < NZ2 - 1).astype(F32)

    def beside2(ref, p):
        c = ref[p]
        around = (
            ref[p + 1]
            + ref[p - 1]
            + (pltpu.roll(c, 1, 0) + pltpu.roll(c, Y2 - 1, 0))
            + (pltpu.roll(c, 1, 1) * not_first + pltpu.roll(c, NZ2 - 1, 1) * not_last)
        )
        return c, around

    def start2(p, c):
        w[PAD2 + p] = g[PAD2 + p] * (16.0 / 9.0)
        return c

    lax.fori_loop(0, NX2, start2, 0, unroll=8)

    def sweep2(p, c):
        centre, around = beside2(w, PAD2 + p)
        r[PAD2 + p] = centre * (4.0 / 3.0) + around * (1.0 / 9.0)
        return c

    lax.fori_loop(0, NX2, sweep2, 0, unroll=8)

    def residue2(q, c):
        total = None
        for i in range(2):
            p = PAD2 + 2 * q + i
            centre, around = beside2(r, p)
            res = g[p] - (6.0 * centre - around) * (1.0 / 16.0)
            total = res if total is None else total + res
        f3[pl.ds(pl.multiple_of(q * Y2, Y2), Y2), :] = total
        return c

    lax.fori_loop(0, NX3, residue2, 0, unroll=4)
    z_sums = dot_right(f3[...], lane_halves(NZ3))
    n3 = NX3 * NY3
    ri = lax.broadcasted_iota(I32, (n3, 2 * n3), 0)
    ci = lax.broadcasted_iota(I32, (n3, 2 * n3), 1)
    source = dot_left(((ci >> 1) == ri).astype(F32) * 0.125, z_sums)
    modes = dot3(dot3(txy_t[...], source), tz[...]) * scale[...]
    solved = dot3(txy[...], dot3(modes, tz[...]))
    rr = lax.broadcasted_iota(I32, (NZ3, NZ2), 0)
    cc = lax.broadcasted_iota(I32, (NZ3, NZ2), 1)
    wide = dot_right(solved, ((cc >> 1) == rr).astype(F32))
    tall = dot_left(((lax.broadcasted_iota(I32, (2 * n3, n3), 0) >> 1) == lax.broadcasted_iota(I32, (2 * n3, n3), 1)).astype(F32), wide)
    f3[...] = tall

    def add_coarse(q, c):
        for i in range(2):
            p = PAD2 + 2 * q + i
            r[p] = r[p] + f3[pl.ds(pl.multiple_of(q * Y2, Y2), Y2), :]
        return c

    lax.fori_loop(0, NX3, add_coarse, 0, unroll=4)
    first2 = 2 * dom

    def post2(src, dst, n, skip):
        for p in range(n):
            q = first2 + skip + p
            centre, around = beside2(src, q)
            new = (3.0 * centre + around + 16.0 * g[q]) * (1.0 / 9.0)
            dst[q] = new * x_ok(q - PAD2, NX2)

    post2(r, w, 8, 1)
    post2(w, r, 6, 2)
    lane = lanes_of((NZ2, LANES))
    signed = jnp.where(lane < 96, lane, lane - LANES)
    place_z = ((grp * Z1 + signed) >> 1 == rows_of((NZ2, LANES))).astype(F32)
    f1[0:3] = f1_lo[...]
    f1[3:11] = f1_own[...]
    f1[11:14] = f1_hi[...]
    mask1 = z_mask(LANES, Z1, grp, NGRP * Z1)

    def ok1(p):
        return mask1 * x_ok(dom * X1 + p - 5, NDOM * X1)

    for p in range(14):
        b1[p] = f1[p] * (4.0 / 9.0)
    level2 = dot_right(r[pl.ds(first2 + 2, 6)].reshape(6 * Y2, NZ2), place_z)
    tall2 = dot_left(doubles(6 * Y2), level2)
    fine = [tall2[p * Y1 : (p + 1) * Y1, :] for p in range(6)]
    for p in range(1, 13):
        centre, around = beside(b1, p)
        new = centre * (4.0 / 3.0) + around * (1.0 / 9.0)
        a1[p] = new * ok1(p) + fine[(p - 1) // 2] * mask1
    for p in range(2, 12):
        centre, around = beside(a1, p)
        b1[p] = (3.0 * centre + around + 4.0 * f1[p]) * (1.0 / 9.0) * ok1(p)
    for p in range(3, 11):
        centre, around = beside(b1, p)
        s1[(p - 3) * Y1 : (p - 2) * Y1, :] = (
            (3.0 * centre + around + 4.0 * f1[p]) * (1.0 / 9.0) * ok1(p)
        )
    r0 = lax.broadcasted_iota(I32, (LANES, W0), 0)
    c0 = lax.broadcasted_iota(I32, (LANES, W0), 1)
    spread0 = dot_right(s1[...], ((c0 >> 1) == r0).astype(F32))
    double_y0 = doubles(Y1)
    for q in range(8):
        ext[q] = dot_left(double_y0, spread0[q * Y1 : (q + 1) * Y1, :])
    mask = z_mask(W0, CZ, grp, NGRP * CZ)
    mask = (mask[:, :LANES], mask[:, LANES:])
    mask9 = [m * (1.0 / 9.0) for m in mask]

    def source(p, h, row):
        return f[p, h, row : row + PART, :]

    def add_fine(p, c):
        for h in range(2):
            fine0 = ext[(p + 1) >> 1, :, h * LANES : (h + 1) * LANES]
            put(e, p, h, u2[p, h] + fine0 * mask[h])
        return c

    lax.fori_loop(0, 14, add_fine, 0, unroll=2)

    def last1(p, c):
        sweep0(e, e2, source, p, 1, 0, mask9, x_ok(dom * CX + p - 2, NDOM * CX))
        return c

    lax.fori_loop(0, 12, last1, 0, unroll=4)

    def last2(p, c):
        sweep0(e2, e, source, p, 1, 1, mask9, x_ok(dom * CX + p - 1, NDOM * CX))
        return c

    lax.fori_loop(0, 10, last2, 0, unroll=5)

    def sums(x, carry):
        p = x + 1
        own = whole(e, p, 0)
        potential[x] = own
        gx = 0.5 * (whole(e, p + 1, 0) - whole(e, p - 1, 0))
        gy = 0.5 * (moved(e, p, 0, 1) - moved(e, p, 0, -1))
        (up, down), _ = z_sides(own, whole(e, p, 1))
        gz = 0.5 * (up - down)
        density = f[x + 2, 0]
        new = (gx * gx, gy * gy, gz * gz, gy * gz, gx * gz, gx * gy, own * density)
        return tuple(
            s + jnp.sum(v.reshape(8, 8, LANES), axis=0) for s, v in zip(carry, new)
        )

    zero = jnp.zeros((8, LANES), F32)
    parts = lax.fori_loop(0, CX, sums, (zero,) * 7, unroll=4)
    lane8 = lanes_of((1, LANES))
    line = jnp.zeros((1, LANES), F32)
    for i, part in enumerate(parts):
        line = jnp.where(lane8 == i, jnp.sum(part), line)
    totals[...] = jnp.broadcast_to(line, (NDEV, LANES))


def after(place, got, f1_own, f1_lo, f1_hi, u2, f):
    consts = [jnp.asarray(t) for t in tables()]
    return pl.pallas_call(
        after_kernel,
        out_shape=(sds(CX, CY, CZ), sds(NDEV, LANES)),
        in_specs=[SM] + [VM] * 10,
        out_specs=(VM, VM),
        scratch_shapes=[
            pltpu.VMEM((NX2 + 2 * PAD2, Y2, NZ2), F32),
            pltpu.VMEM((NX2 + 2 * PAD2, Y2, NZ2), F32),
            pltpu.VMEM((NX2 + 2 * PAD2, Y2, NZ2), F32),
            pltpu.VMEM((NX3 * Y2, NZ2), F32),
            pltpu.VMEM((14 * 2 * STEP, LANES), F32),
            pltpu.VMEM((12 * 2 * STEP, LANES), F32),
            pltpu.VMEM((14, Y1, LANES), F32),
            pltpu.VMEM((14, Y1, LANES), F32),
            pltpu.VMEM((14, Y1, LANES), F32),
            pltpu.VMEM((8, CY, W0), F32),
            pltpu.VMEM((8 * Y1, LANES), F32),
        ],
        input_output_aliases={},
        compiler_params=PAR,
        name="after",
    )(place, got, *consts, f1_own, f1_lo, f1_hi, u2, f)


def stress_kernel(got, out):
    total = jnp.sum(got[...], axis=0, keepdims=True)
    lane = lanes_of((1, LANES))
    energy = jnp.sum(jnp.where(lane == 6, total, 0.0))
    cells = float(NDOM * CX * CY * NGRP * CZ)
    line = total / cells - jnp.where(lane < 3, 0.5 * energy / cells, 0.0)
    out[...] = line[0, :6]


def stress_of(got):
    return pl.pallas_call(
        stress_kernel,
        out_shape=sds(6),
        in_specs=[VM],
        out_specs=VM,
        name="stress",
    )(got)


def shift(value, axis, distance):
    n = lax.axis_size(axis)
    route = [(i, i + distance) for i in range(n) if 0 <= i + distance < n]
    return lax.ppermute(value, axis, route)


def step(valence, start, tiles, home, ox, oy, oz, size):
    place = jnp.stack([lax.axis_index(DOM), lax.axis_index(GRP)]).astype(I32)
    lower = shift(start[CX - HU :], DOM, 1)
    upper = shift(start[:HU], DOM, -1)
    message = pack_atoms([v.reshape(-1) for v in (home, ox, oy, oz, size)], tiles)
    got = lax.all_to_all(message.reshape(NDEV, ROWS * LANES), ALL, 0, 0, tiled=True)
    got = got.reshape(NDEV * ROWS, LANES)
    u_left, u_right = edges(start, lower, upper)
    grid, up2, down = deposit(got, valence)
    from1 = shift(grid[2 * CY : 15 * CY].reshape(13, CY, LANES), DOM, 1)
    from2 = shift(up2.reshape(5, CY, LANES), DOM, 2)
    above = shift(down.reshape(6, CY, LANES), DOM, -1)
    u_from_right = shift(u_left, GRP, -1)
    u_from_left = shift(u_right, GRP, 1)
    f, left, right = join(
        grid, from1, from2, above
    )
    from_right = shift(left, GRP, -1)
    from_left = shift(right, GRP, 1)
    u2, fe, f1, chunk = before(
        place, f, lower, start, upper, u_from_left, u_from_right, from_left, from_right
    )
    f1_lo = shift(f1[1:4], DOM, 1)
    f1_hi = shift(f1[4:7], DOM, -1)
    chunks = jnp.broadcast_to(chunk[None], (NDEV, 8, LANES))
    everything = lax.all_to_all(chunks, ALL, 0, 0, tiled=True)
    potential, totals = after(place, everything, f1, f1_lo, f1_hi, u2, fe)
    sums = lax.all_to_all(totals, ALL, 0, 0, tiled=True)
    return potential, stress_of(sums)


def solution(mesh):
    split = Mesh(mesh.devices.reshape(4, 4, 4, 2), ("dom_0", "dom_1", "grp_0", "grp_1"))
    atoms = P(DOM + GRP, None)
    return jax.shard_map(
        step,
        mesh=split,
        in_specs=(P(DOM, None, GRP), P(DOM, None, GRP)) + (atoms,) * 6,
        out_specs=(P(DOM, None, GRP), P()),
        check_vma=False,
    )
```

```python
import functools

import jax
import jax.numpy as jnp
import numpy as np
from jax import lax
from jax.experimental import pallas as pl
from jax.experimental.pallas import tpu as pltpu
from jax.sharding import Mesh
from jax.sharding import PartitionSpec as P


CAP = 4
DOM = ("dom_0", "dom_1")
GRP = ("grp_0", "grp_1")
ALL = DOM + GRP
F32 = jnp.float32
I32 = jnp.int32
VM = pl.BlockSpec(memory_space=pltpu.VMEM)
SM = pl.BlockSpec(memory_space=pltpu.SMEM)

CX, CY, CZ = 8, 64, 128
NDOM, NGRP = 16, 8
NDEV = NDOM * NGRP
ATOMS = 256
TILE_ROWS = 4
LANES = 128
PAR = pltpu.CompilerParams(vmem_limit_bytes=16 * 1024 * 1024)


def sds(*shape, dtype=F32):
    return jax.ShapeDtypeStruct(shape, dtype)


def lanes_of(shape):
    return lax.broadcasted_iota(I32, shape, len(shape) - 1)


def rows_of(shape):
    return lax.broadcasted_iota(I32, shape, len(shape) - 2)


def split(a):
    hi = a.astype(jnp.bfloat16)
    return hi, (a - hi.astype(F32)).astype(jnp.bfloat16)


def dot3(a, b):
    (ah, al), (bh, bl) = split(a), split(b)
    low = jnp.dot(ah, bl, preferred_element_type=F32) + jnp.dot(al, bh, preferred_element_type=F32)
    return jnp.dot(ah, bh, preferred_element_type=F32) + low


def dot_right(a, ones):
    hi = a.astype(jnp.bfloat16)
    lo = (a - hi.astype(F32)).astype(jnp.bfloat16)
    ones = ones.astype(jnp.bfloat16)
    return jnp.dot(hi, ones, preferred_element_type=F32) + jnp.dot(
        lo, ones, preferred_element_type=F32
    )


def dot_left(ones, a):
    hi = a.astype(jnp.bfloat16)
    lo = (a - hi.astype(F32)).astype(jnp.bfloat16)
    ones = ones.astype(jnp.bfloat16)
    return jnp.dot(ones, hi, preferred_element_type=F32) + jnp.dot(
        ones, lo, preferred_element_type=F32
    )


ROWS = CAP * TILE_ROWS + 1


def pack_kernel(
    home_h, ox_h, oy_h, oz_h, size_h, tiles_h, out, rows, count, home, ox, oy, oz, size, tiles, sem
):
    copies = [
        pltpu.make_async_copy(src, dst, sem.at[i])
        for i, (src, dst) in enumerate(
            ((home_h, home), (ox_h, ox), (oy_h, oy), (oz_h, oz), (size_h, size), (tiles_h, tiles))
        )
    ]
    for copy in copies:
        copy.start()

    def clear_out(i, c):
        out[pl.ds(pl.multiple_of(i * 8, 8), 8), :] = jnp.zeros((8, LANES), F32)
        return c

    lax.fori_loop(0, NDEV * ROWS // 8, clear_out, 0, unroll=8)

    def clear(i, c):
        count[i] = 0
        return c

    lax.fori_loop(0, NDEV, clear, 0, unroll=8)
    copies[5].wait()
    lower = lanes_of((8, LANES)) < 64
    for g in range(ATOMS // 8):
        old = [tiles[g * 8 : g * 8 + 8, r * LANES : (r + 1) * LANES] for r in range(4)]
        turned = [pltpu.roll(v, 64, 1) for v in old]
        new = (
            jnp.where(lower, old[0], turned[2]),
            jnp.where(lower, turned[0], old[2]),
            jnp.where(lower, old[1], turned[3]),
            jnp.where(lower, turned[1], old[3]),
        )
        for r in range(TILE_ROWS):
            rows[pl.ds(g * 8 * TILE_ROWS + r, 8, stride=TILE_ROWS), :] = new[r]

    for copy in copies[:5]:
        copy.wait()
    lane = lanes_of((TILE_ROWS, LANES))
    need = rows_of((TILE_ROWS, LANES)) + jnp.where(lane < 64, 0, 4)
    need = jnp.maximum(jnp.maximum(need, (lane >> 3) & 7), lane & 7)
    tile_c = lane & 7
    part1, slot1 = lanes_of((1, LANES)) & 3, lanes_of((1, LANES)) >> 2

    for start in range(0, ATOMS, PER_STEP):
        placed = []
        for n in range(start, start + PER_STEP):
            z_in = oz[n] & 7
            shift_ = (oy[n] & 15) * 8 + z_in
            value = rows[n * TILE_ROWS : (n + 1) * TILE_ROWS, :]
            value = jnp.where(need < size[n], value, 0.0)
            near = pltpu.roll(value, shift_, 1)
            far = pltpu.roll(value, shift_ + 120, 1)
            placed.append(jnp.where(tile_c >= z_in, near, far))
        for n in range(start, start + PER_STEP):
            to = home[n]
            rank = count[to]
            count[to] = rank + 1
            base = to * ROWS
            out[pl.ds(base + rank * TILE_ROWS, TILE_ROWS), :] = placed[n - start]
            line = jnp.where(part1 == 0, ox[n], jnp.where(part1 == 1, oy[n], oz[n]))
            pltpu.store(
                out.at[pl.ds(base + ROWS - 1, 1), :], line.astype(F32), mask=slot1 == rank
            )


PER_STEP = 16


def pack_atoms(scalars, tiles):
    return pl.pallas_call(
        pack_kernel,
        out_shape=sds(NDEV * ROWS, LANES),
        in_specs=[pl.BlockSpec(memory_space=pl.ANY)] * 6,
        out_specs=VM,
        scratch_shapes=[
            pltpu.VMEM((ATOMS * TILE_ROWS, LANES), F32),
            pltpu.SMEM((NDEV,), I32),
        ]
        + [pltpu.SMEM((ATOMS,), I32)] * 5
        + [pltpu.VMEM((ATOMS, TILE_ROWS * LANES), F32), pltpu.SemaphoreType.DMA((6,))],
        name="pack_atoms",
    )(*scalars, tiles)


ZB = CZ // 8 + 1
YB = 4


def deposit_kernel(got, valence, grid, up2, down, acc_a, acc_b, other, corner_v, corner_s, sem):
    part = lanes_of((8, LANES)) & 3
    for g in range(NDEV // 8):
        raw = got[pl.ds(g * 8 * ROWS + ROWS - 1, 8, stride=ROWS), :].astype(I32)
        back, ahead, ahead2 = (pltpu.roll(raw, n, 1) for n in (1, 127, 126))
        x = jnp.where(part == 0, raw, back)
        y = jnp.where(part == 0, ahead, jnp.where(part == 1, raw, back))
        z = jnp.where(part == 0, ahead2, jnp.where(part == 1, ahead, back))
        y_block = jnp.where(part == 1, ((y >> 4) + 1) & 3, y >> 4)
        row = (y_block * ZB + (z >> 3)) * 16 + x
        corner_v[g * 8 : g * 8 + 8, :] = jnp.where(
            part < 2, row, jnp.where(part == 2, (y & 15) * 8, z & 7)
        )
    copy = pltpu.make_async_copy(corner_v, corner_s, sem)
    copy.start()

    def turn(i, c):
        at = pl.ds(pl.multiple_of(i * 32, 8), 32)
        other[at, :] = pltpu.roll(got[at, :], 64, 1)
        return c

    lax.fori_loop(0, NDEV * ROWS // 32, turn, 0, unroll=4)

    def clear(i, c):
        zero = jnp.zeros((16, LANES), F32)
        acc_a[pl.ds(pl.multiple_of(i * 16, 16), 16), :] = zero
        acc_b[pl.ds(pl.multiple_of(i * 16, 16), 16), :] = zero
        return c

    lax.fori_loop(0, YB * ZB, clear, 0, unroll=4)
    copy.wait()
    lane = lanes_of((8, LANES))
    z_of = lane & 7

    for src in range(NDEV):
        for k in range(CAP):
            acc = acc_a if k % 2 == 0 else acc_b
            row = corner_s[src, 4 * k]
            wrapped = corner_s[src, 4 * k + 1]
            first = corner_s[src, 4 * k + 2]
            z_in = corner_s[src, 4 * k + 3]
            at = pl.ds(src * ROWS + k * TILE_ROWS, TILE_ROWS)
            value = jnp.concatenate([got[at, :], other[at, :]], axis=0)
            same = (lane >= first) & (lane < first + 64)
            here = jnp.where(same, value, 0.0)
            round_ = jnp.where(lane < first - 64, value, 0.0)
            near = z_of >= z_in
            a0 = acc[pl.ds(row, 8), :]
            a1 = acc[pl.ds(row + 16, 8), :]
            a2 = acc[pl.ds(wrapped, 8), :]
            a3 = acc[pl.ds(wrapped + 16, 8), :]
            acc[pl.ds(row, 8), :] = a0 + jnp.where(near, here, 0.0)
            acc[pl.ds(row + 16, 8), :] = a1 + jnp.where(near, 0.0, here)
            acc[pl.ds(wrapped, 8), :] = a2 + jnp.where(near, round_, 0.0)
            acc[pl.ds(wrapped + 16, 8), :] = a3 + jnp.where(near, 0.0, round_)
    group = lane >> 3

    def lay_out(yb, c):
        for xg in range(2):
            blocks = []
            for zb in range(CZ // 8):
                at = pl.ds(pl.multiple_of((yb * ZB + zb) * 16 + xg * 8, 8), 8)
                blocks.append(acc_a[at, :] + acc_b[at, :])
            for s in (8, 4, 2, 1):
                low = (group & s) == 0
                for i in range(16):
                    if i & s == 0:
                        one_, two = blocks[i], blocks[i + s]
                        blocks[i] = jnp.where(low, one_, pltpu.roll(two, 8 * s, 1))
                        blocks[i + s] = jnp.where(low, pltpu.roll(one_, 128 - 8 * s, 1), two)
            for yy in range(16):
                grid[pl.ds(xg * 8 * CY + yb * 16 + yy, 8, stride=CY), :] = blocks[yy]
        return c

    lax.fori_loop(0, YB, lay_out, 0)
    grid[0 : CX * CY, :] += valence[...]
    up2[...] = grid[10 * CY : 15 * CY, :]
    down[...] = grid[0 : 6 * CY, :]


def deposit(got, valence):
    return pl.pallas_call(
        deposit_kernel,
        out_shape=(sds(16 * CY, LANES), sds(5 * CY, LANES), sds(6 * CY, LANES)),
        in_specs=[VM, VM],
        out_specs=(VM, VM, VM),
        scratch_shapes=[
            pltpu.VMEM((YB * ZB * 16, LANES), F32),
            pltpu.VMEM((YB * ZB * 16, LANES), F32),
            pltpu.VMEM((NDEV * ROWS, LANES), F32),
            pltpu.VMEM((NDEV, LANES), I32),
            pltpu.SMEM((NDEV, LANES), I32),
            pltpu.SemaphoreType.DMA,
        ],
        compiler_params=PAR,
        name="deposit",
    )(got, valence.reshape(CX * CY, LANES))


HU, HF = 7, 6
NU_, NF = CX + 2 * HU, CX + 2 * HF
UGROUPS, FGROUPS = -(-NU_ // 8), -(-NF // 8)


def u_plane(p, u_lo, start, u_hi):
    if p < HU:
        return u_lo[p]
    return start[p - HU] if p < HU + CX else u_hi[p - HU - CX]


def pack_edges(planes, left, right, at):
    slot = lanes_of((CY, LANES)) >> 4
    for g in range(-(-len(planes) // 8)):
        lo = jnp.zeros((CY, LANES), F32)
        hi = jnp.zeros((CY, LANES), F32)
        for k, plane in enumerate(planes[g * 8 : g * 8 + 8]):
            plane = plane()
            plane = pltpu.roll(plane, 16 * k, 1) if k else plane
            lo = jnp.where(slot == k, plane, lo)
            hi = jnp.where(slot == (k - 1) % 8, plane, hi)
        left[at + g] = lo
        right[at + g] = hi


def own_edges_kernel(start, left, right):
    pack_edges([functools.partial(lambda q: start[q], p) for p in range(CX)], left, right, 0)


def own_edges(start):
    return pl.pallas_call(
        own_edges_kernel,
        out_shape=(sds(1, CY, LANES),) * 2,
        in_specs=[VM],
        out_specs=(VM,) * 2,
        compiler_params=PAR,
        name="own_edges",
    )(start)


def edges_kernel(own_left, own_right, u_lo, u_hi, left, right):
    left[0] = own_left[0]
    right[0] = own_right[0]
    pack_edges([functools.partial(lambda q: u_lo[q], p) for p in range(HU)], left, right, 1)
    pack_edges([functools.partial(lambda q: u_hi[q], p) for p in range(HU)], left, right, 2)


def edges(own_left, own_right, u_lo, u_hi):
    return pl.pallas_call(
        edges_kernel,
        out_shape=(sds(UGROUPS, CY, LANES),) * 2,
        in_specs=[VM] * 4,
        out_specs=(VM,) * 2,
        compiler_params=PAR,
        name="edges",
    )(own_left, own_right, u_lo, u_hi)


def join_kernel(grid, from1, from2, above, f, left, right):
    for p in range(NF):
        x = p - HF
        if x < 0:
            total = from1[x + 6]
            if x < -1:
                total = total + from2[x + 6]
        elif x < CX:
            total = grid[x * CY : (x + 1) * CY, :]
            if x < 7:
                total = total + from1[x + 6]
        else:
            total = above[x - CX]
            if x < 15:
                total = total + grid[x * CY : (x + 1) * CY, :]
        f[p] = total
    pack_edges([functools.partial(lambda q: f[q], p) for p in range(NF)], left, right, 0)


def join(*args):
    return pl.pallas_call(
        join_kernel,
        out_shape=(
            sds(NF, CY, LANES),
            sds(FGROUPS, CY, LANES),
            sds(FGROUPS, CY, LANES),
        ),
        in_specs=[VM] * 4,
        out_specs=(VM,) * 3,
        compiler_params=PAR,
        name="join",
    )(*args)


W0 = 256
X1, Y1, Z1 = 4, 32, 64
X2, Y2, Z2 = 2, 16, 32


def beside(ref, p):
    c = ref[p]
    n, w = c.shape
    return c, (
        ref[p + 1]
        + ref[p - 1]
        + (pltpu.roll(c, 1, 0) + pltpu.roll(c, n - 1, 0))
        + (pltpu.roll(c, 1, 1) + pltpu.roll(c, w - 1, 1))
    )


def z_mask(width, own, grp, total):
    lane = lanes_of((1, width))
    split = own + (width - own) // 2
    z = grp * own + jnp.where(lane < split, lane, lane - width)
    return ((z >= 0) & (z < total)).astype(F32)


def x_ok(x, total):
    return jnp.where((x >= 0) & (x < total), 1.0, 0.0).astype(F32)


def halves(n):
    r = lax.broadcasted_iota(I32, (n, 2 * n), 0)
    c = lax.broadcasted_iota(I32, (n, 2 * n), 1)
    return ((c >> 1) == r).astype(F32)


def doubles(n):
    r = lax.broadcasted_iota(I32, (2 * n, n), 0)
    c = lax.broadcasted_iota(I32, (2 * n, n), 1)
    return ((r >> 1) == c).astype(F32)


def lane_halves(n):
    r = lax.broadcasted_iota(I32, (2 * n, n), 0)
    c = lax.broadcasted_iota(I32, (2 * n, n), 1)
    return ((r >> 1) == c).astype(F32)


STEP = CY + 16


def half_at(p, h):
    return (p * 2 + h) * STEP


PART = 32


def whole(ref, p, h, row=0, n=CY):
    return ref[pl.ds(pl.multiple_of(half_at(p, h) + 8 + row, 8), n), :]


def put(ref, p, h, value, row=0):
    base = half_at(p, h)
    n = value.shape[0]
    ref[pl.ds(pl.multiple_of(base + 8 + row, 8), n), :] = value
    if row + n == CY:
        ref[pl.ds(pl.multiple_of(base, 8), 8), :] = value[n - 8 :]
    if row == 0:
        ref[pl.ds(pl.multiple_of(base + 8 + CY, 8), 8), :] = value[:8]


def moved(ref, p, h, by, row=0, n=CY):
    return ref[pl.ds(half_at(p, h) + 8 + row + by, n), :]


def z_sides(own, edge):
    lane = lanes_of(own.shape)
    first, last = lane == 0, lane == LANES - 1
    own_up, edge_up = pltpu.roll(own, LANES - 1, 1), pltpu.roll(edge, LANES - 1, 1)
    own_down, edge_down = pltpu.roll(own, 1, 1), pltpu.roll(edge, 1, 1)
    return (
        (jnp.where(last, edge_up, own_up), jnp.where(first, edge_down, own_down)),
        (jnp.where(last, own_up, edge_up), jnp.where(first, own_down, edge_down)),
    )


def beside0(ref, p, row):
    centre = [whole(ref, p, h, row, PART) for h in range(2)]
    sides = z_sides(*centre)
    around = [
        (whole(ref, p + 1, h, row, PART) + whole(ref, p - 1, h, row, PART))
        + (moved(ref, p, h, 1, row, PART) + moved(ref, p, h, -1, row, PART))
        + (sides[h][0] + sides[h][1])
        for h in range(2)
    ]
    return centre, around


def sweep0(src, dst, f, p, shift_u, shift_f, mask, ok):
    for row in range(0, CY, PART):
        centre, around = beside0(src, p + shift_u, row)
        for h in range(2):
            new = 3.0 * centre[h] + around[h] + f(p + shift_f, h, row)
            put(dst, p, h, new * (mask[h] * ok), row)


def before_kernel(
    place, f_in, u_lo, start, u_hi, u_from_left, u_from_right, f_from_left, f_from_right, u_out, f_out, f1, chunk, u, ua, fe, u2, pairs, v1, r1
):
    dom, grp = place[0], place[1]
    slot = lanes_of((CY, LANES)) >> 4
    for p in range(NU_ + NF):
        if p < NU_:
            g, k = (1, p) if p < HU else (0, p - HU) if p < HU + CX else (2, p - HU - CX)
            from_left, from_right = u_from_left, u_from_right
        else:
            g, k, from_left, from_right = (p - NU_) // 8, (p - NU_) % 8, f_from_left, f_from_right
        edge = jnp.where(slot == k, from_right[g], 0.0)
        edge = jnp.where(slot == (k - 1) % 8, from_left[g], edge)
        edge = pltpu.roll(edge, (-16 * k) % 128, 1) if k else edge
        if p < NU_:
            put(u, p, 0, u_plane(p, u_lo, start, u_hi))
            put(u, p, 1, edge)
        else:
            fe[p - NU_] = edge
    f = (f_in, fe)

    def source(p, h, row):
        return f[h][p, row : row + PART, :]

    mask = z_mask(W0, CZ, grp, NGRP * CZ) * (1.0 / 9.0)
    mask = (mask[:, :LANES], mask[:, LANES:])

    def sweep1(p, c):
        sweep0(u, ua, source, p, 1, 0, mask, x_ok(dom * CX + p - HF, NDOM * CX))
        return c

    lax.fori_loop(0, NF, sweep1, 0, unroll=4)

    def sweep2(p, c):
        sweep0(ua, u2, source, p, 1, 1, mask, x_ok(dom * CX + p - 5, NDOM * CX))
        return c

    lax.fori_loop(0, NF - 2, sweep2, 0, unroll=3)

    for p in range(14):
        for h in range(2):
            u_out[p, h] = whole(u2, p + 2, h)
    for p in range(12):
        for h in range(2):
            f_out[p, h] = f[h][p + 4]

    def residue0(q, c):
        for row in range(0, CY, PART):
            total = [None, None]
            for i in range(2):
                p = 2 * q + i + 1
                centre, around = beside0(u2, p, row)
                for h in range(2):
                    r = source(p + 1, h, row) - (6.0 * centre[h] - around[h])
                    total[h] = r if total[h] is None else total[h] + r
            at = pl.ds(pl.multiple_of(q * CY + row, 8), PART)
            for h in range(2):
                pairs[at, h * LANES : (h + 1) * LANES] = total[h]
        return c

    lax.fori_loop(0, 8, residue0, 0, unroll=2)
    summed = dot_right(pairs[...], lane_halves(LANES))
    half_y = halves(Y1) * 0.125
    mask1 = z_mask(LANES, Z1, grp, NGRP * Z1)
    for q in range(8):
        part = dot_left(half_y, summed[q * CY : (q + 1) * CY, :])
        f1[q] = part * (mask1 * x_ok(dom * X1 + q - 2, NDOM * X1))
    for q in range(8):
        v1[q] = f1[q] * (4.0 / 9.0)
    for q in range(1, 7):
        centre, around = beside(v1, q)
        new = centre * (4.0 / 3.0) + around * (1.0 / 9.0)
        r1[q] = new * (mask1 * x_ok(dom * X1 + q - 2, NDOM * X1))
    half_y2 = halves(Y2) * 0.125
    lane_half = lane_halves(LANES // 2)
    rows = []
    for i in range(2):
        total = None
        for j in range(2):
            q = 2 + 2 * i + j
            centre, around = beside(r1, q)
            r = f1[q] - (6.0 * centre - around) * 0.25
            total = r if total is None else total + r
        rows.append(total)
    both = dot_right(jnp.concatenate(rows, axis=0), jnp.concatenate([lane_half, jnp.zeros_like(lane_half)], axis=1))
    packed = jnp.zeros((8, LANES), F32)
    slot = lanes_of((8, LANES)) >> 5
    for i in range(2):
        part = dot_left(half_y2, both[i * Y1 : (i + 1) * Y1, :])
        for yb in range(2):
            s = 2 * i + yb
            piece = part[yb * 8 : yb * 8 + 8, :]
            piece = pltpu.roll(piece, 32 * s, 1) if s else piece
            packed = jnp.where(slot == s, piece, packed)

    packed = pltpu.roll(packed, (grp & 3) * 32, 1)
    chunk[...] = packed


def before(place, *args):
    return pl.pallas_call(
        before_kernel,
        out_shape=(
            sds(14, 2, CY, LANES),
            sds(12, 2, CY, LANES),
            sds(8, Y1, LANES),
            sds(8, LANES),
        ),
        in_specs=[SM] + [VM] * 8,
        out_specs=(VM,) * 4,
        scratch_shapes=[
            pltpu.VMEM((NU_ * 2 * STEP, LANES), F32),
            pltpu.VMEM((NF * 2 * STEP, LANES), F32),
            pltpu.VMEM((NF, CY, LANES), F32),
            pltpu.VMEM(((NF - 2) * 2 * STEP, LANES), F32),
            pltpu.VMEM((8 * CY, W0), F32),
            pltpu.VMEM((8, Y1, LANES), F32),
            pltpu.VMEM((8, Y1, LANES), F32),
        ],
        compiler_params=PAR,
        name="before",
    )(place, *args)


NX2, NZ2 = NDOM * X2, NGRP * Z2
NX3, NY3, NZ3 = NX2 // 2, Y2 // 2, NZ2 // 2
PAD2 = 4


def tables():
    def sine(n):
        k = np.arange(n) + 1.0
        t = np.sqrt(2.0 / (n + 1)) * np.sin(np.pi * np.outer(k, k) / (n + 1))
        return t, 2.0 - 2.0 * np.cos(np.pi * k / (n + 1))

    def cyclic(n):
        j = np.arange(n)[:, None]
        col = np.arange(n)[None, :]
        freq = (col + 1) // 2
        angle = 2.0 * np.pi * freq * j / n
        use_sine = (col % 2 == 0) & (col > 0)
        edge = (col == 0) | (col == n - 1)
        t = np.where(edge, np.sqrt(1.0 / n), np.sqrt(2.0 / n)) * np.where(
            use_sine, np.sin(angle), np.cos(angle)
        )
        return t, 2.0 - 2.0 * np.cos(2.0 * np.pi * freq[0] / n)

    tx, lx = sine(NX3)
    ty, ly = cyclic(NY3)
    tz, lz = sine(NZ3)
    txy = np.kron(tx, ty)
    lxy = (lx[:, None] + ly[None, :]).reshape(-1)
    scale = 64.0 / (lxy[:, None] + lz[None, :])
    return tuple(np.asarray(a, np.float32) for a in (txy, np.ascontiguousarray(txy.T), tz, scale))


def after_kernel(
    place, got, txy, txy_t, tz, scale, f1_own, f1_lo, f1_hi, u2, f,
    potential, totals, g, w, r, f3, e, e2, a1, b1, f1, ext, s1,
):
    dom, grp = place[0], place[1]
    zero2 = jnp.zeros((Y2, NZ2), F32)
    for p in range(PAD2):
        g[p] = zero2
        g[PAD2 + NX2 + p] = zero2
        w[p] = zero2
        w[PAD2 + NX2 + p] = zero2
        r[p] = zero2
        r[PAD2 + NX2 + p] = zero2
    slot = lanes_of((8, LANES)) >> 5

    def gather(d, c):
        for i in range(2):
            for yb in range(2):
                s = 2 * i + yb
                for t in range(2):
                    row = None
                    for q in range(4):
                        piece = got[d * NGRP + 4 * t + q]
                        row = piece if row is None else jnp.where(slot == (s + q) % 4, piece, row)
                    row = pltpu.roll(row, (-32 * s) % 128, 1) if s else row
                    g[PAD2 + 2 * d + i, yb * 8 : yb * 8 + 8, t * LANES : (t + 1) * LANES] = row
        return c

    lax.fori_loop(0, NDOM, gather, 0, unroll=4)
    lane2 = lanes_of((1, NZ2))
    not_first = (lane2 > 0).astype(F32)
    not_last = (lane2 < NZ2 - 1).astype(F32)

    def beside2(ref, p):
        c = ref[p]
        around = (
            ref[p + 1]
            + ref[p - 1]
            + (pltpu.roll(c, 1, 0) + pltpu.roll(c, Y2 - 1, 0))
            + (pltpu.roll(c, 1, 1) * not_first + pltpu.roll(c, NZ2 - 1, 1) * not_last)
        )
        return c, around

    def start2(p, c):
        w[PAD2 + p] = g[PAD2 + p] * (16.0 / 9.0)
        return c

    lax.fori_loop(0, NX2, start2, 0, unroll=8)

    def sweep2(p, c):
        centre, around = beside2(w, PAD2 + p)
        r[PAD2 + p] = centre * (4.0 / 3.0) + around * (1.0 / 9.0)
        return c

    lax.fori_loop(0, NX2, sweep2, 0, unroll=8)

    def residue2(q, c):
        total = None
        for i in range(2):
            p = PAD2 + 2 * q + i
            centre, around = beside2(r, p)
            res = g[p] - (6.0 * centre - around) * (1.0 / 16.0)
            total = res if total is None else total + res
        f3[pl.ds(pl.multiple_of(q * Y2, Y2), Y2), :] = total
        return c

    lax.fori_loop(0, NX3, residue2, 0, unroll=4)
    z_sums = dot_right(f3[...], lane_halves(NZ3))
    n3 = NX3 * NY3
    ri = lax.broadcasted_iota(I32, (n3, 2 * n3), 0)
    ci = lax.broadcasted_iota(I32, (n3, 2 * n3), 1)
    source = dot_left(((ci >> 1) == ri).astype(F32) * 0.125, z_sums)
    modes = dot3(dot3(txy_t[...], source), tz[...]) * scale[...]
    solved = dot3(txy[...], dot3(modes, tz[...]))
    rr = lax.broadcasted_iota(I32, (NZ3, NZ2), 0)
    cc = lax.broadcasted_iota(I32, (NZ3, NZ2), 1)
    wide = dot_right(solved, ((cc >> 1) == rr).astype(F32))
    tall = dot_left(((lax.broadcasted_iota(I32, (2 * n3, n3), 0) >> 1) == lax.broadcasted_iota(I32, (2 * n3, n3), 1)).astype(F32), wide)
    f3[...] = tall

    def add_coarse(q, c):
        for i in range(2):
            p = PAD2 + 2 * q + i
            r[p] = r[p] + f3[pl.ds(pl.multiple_of(q * Y2, Y2), Y2), :]
        return c

    lax.fori_loop(0, NX3, add_coarse, 0, unroll=4)
    first2 = 2 * dom

    def post2(src, dst, n, skip):
        for p in range(n):
            q = first2 + skip + p
            centre, around = beside2(src, q)
            new = (3.0 * centre + around + 16.0 * g[q]) * (1.0 / 9.0)
            dst[q] = new * x_ok(q - PAD2, NX2)

    post2(r, w, 8, 1)
    post2(w, r, 6, 2)
    lane = lanes_of((NZ2, LANES))
    signed = jnp.where(lane < 96, lane, lane - LANES)
    place_z = ((grp * Z1 + signed) >> 1 == rows_of((NZ2, LANES))).astype(F32)
    f1[0:3] = f1_lo[...]
    f1[3:11] = f1_own[...]
    f1[11:14] = f1_hi[...]
    mask1 = z_mask(LANES, Z1, grp, NGRP * Z1)

    def ok1(p):
        return mask1 * x_ok(dom * X1 + p - 5, NDOM * X1)

    for p in range(14):
        b1[p] = f1[p] * (4.0 / 9.0)
    level2 = dot_right(r[pl.ds(first2 + 2, 6)].reshape(6 * Y2, NZ2), place_z)
    tall2 = dot_left(doubles(6 * Y2), level2)
    fine = [tall2[p * Y1 : (p + 1) * Y1, :] for p in range(6)]
    for p in range(1, 13):
        centre, around = beside(b1, p)
        new = centre * (4.0 / 3.0) + around * (1.0 / 9.0)
        a1[p] = new * ok1(p) + fine[(p - 1) // 2] * mask1
    for p in range(2, 12):
        centre, around = beside(a1, p)
        b1[p] = (3.0 * centre + around + 4.0 * f1[p]) * (1.0 / 9.0) * ok1(p)
    for p in range(3, 11):
        centre, around = beside(b1, p)
        s1[(p - 3) * Y1 : (p - 2) * Y1, :] = (
            (3.0 * centre + around + 4.0 * f1[p]) * (1.0 / 9.0) * ok1(p)
        )
    r0 = lax.broadcasted_iota(I32, (LANES, W0), 0)
    c0 = lax.broadcasted_iota(I32, (LANES, W0), 1)
    spread0 = dot_right(s1[...], ((c0 >> 1) == r0).astype(F32))
    double_y0 = doubles(Y1)
    for q in range(8):
        ext[q] = dot_left(double_y0, spread0[q * Y1 : (q + 1) * Y1, :])
    mask = z_mask(W0, CZ, grp, NGRP * CZ)
    mask = (mask[:, :LANES], mask[:, LANES:])
    mask9 = [m * (1.0 / 9.0) for m in mask]

    def source(p, h, row):
        return f[p, h, row : row + PART, :]

    def add_fine(p, c):
        for h in range(2):
            fine0 = ext[(p + 1) >> 1, :, h * LANES : (h + 1) * LANES]
            put(e, p, h, u2[p, h] + fine0 * mask[h])
        return c

    lax.fori_loop(0, 14, add_fine, 0, unroll=2)

    def last1(p, c):
        sweep0(e, e2, source, p, 1, 0, mask9, x_ok(dom * CX + p - 2, NDOM * CX))
        return c

    lax.fori_loop(0, 12, last1, 0, unroll=4)

    def last2(p, c):
        sweep0(e2, e, source, p, 1, 1, mask9, x_ok(dom * CX + p - 1, NDOM * CX))
        return c

    lax.fori_loop(0, 10, last2, 0, unroll=5)

    def sums(x, carry):
        p = x + 1
        own = whole(e, p, 0)
        potential[x] = own
        gx = 0.5 * (whole(e, p + 1, 0) - whole(e, p - 1, 0))
        gy = 0.5 * (moved(e, p, 0, 1) - moved(e, p, 0, -1))
        (up, down), _ = z_sides(own, whole(e, p, 1))
        gz = 0.5 * (up - down)
        density = f[x + 2, 0]
        new = (gx * gx, gy * gy, gz * gz, gy * gz, gx * gz, gx * gy, own * density)
        return tuple(
            s + jnp.sum(v.reshape(8, 8, LANES), axis=0) for s, v in zip(carry, new)
        )

    zero = jnp.zeros((8, LANES), F32)
    parts = lax.fori_loop(0, CX, sums, (zero,) * 7, unroll=4)
    lane8 = lanes_of((1, LANES))
    line = jnp.zeros((1, LANES), F32)
    for i, part in enumerate(parts):
        line = jnp.where(lane8 == i, jnp.sum(part), line)
    totals[...] = jnp.broadcast_to(line, (NDEV, LANES))


def after(place, got, f1_own, f1_lo, f1_hi, u2, f):
    consts = [jnp.asarray(t) for t in tables()]
    return pl.pallas_call(
        after_kernel,
        out_shape=(sds(CX, CY, CZ), sds(NDEV, LANES)),
        in_specs=[SM] + [VM] * 10,
        out_specs=(VM, VM),
        scratch_shapes=[
            pltpu.VMEM((NX2 + 2 * PAD2, Y2, NZ2), F32),
            pltpu.VMEM((NX2 + 2 * PAD2, Y2, NZ2), F32),
            pltpu.VMEM((NX2 + 2 * PAD2, Y2, NZ2), F32),
            pltpu.VMEM((NX3 * Y2, NZ2), F32),
            pltpu.VMEM((14 * 2 * STEP, LANES), F32),
            pltpu.VMEM((12 * 2 * STEP, LANES), F32),
            pltpu.VMEM((14, Y1, LANES), F32),
            pltpu.VMEM((14, Y1, LANES), F32),
            pltpu.VMEM((14, Y1, LANES), F32),
            pltpu.VMEM((8, CY, W0), F32),
            pltpu.VMEM((8 * Y1, LANES), F32),
        ],
        input_output_aliases={},
        compiler_params=PAR,
        name="after",
    )(place, got, *consts, f1_own, f1_lo, f1_hi, u2, f)


def stress_kernel(got, out):
    total = jnp.sum(got[...], axis=0, keepdims=True)
    lane = lanes_of((1, LANES))
    energy = jnp.sum(jnp.where(lane == 6, total, 0.0))
    cells = float(NDOM * CX * CY * NGRP * CZ)
    line = total / cells - jnp.where(lane < 3, 0.5 * energy / cells, 0.0)
    out[...] = line[0, :6]


def stress_of(got):
    return pl.pallas_call(
        stress_kernel,
        out_shape=sds(6),
        in_specs=[VM],
        out_specs=VM,
        name="stress",
    )(got)


def shift(value, axis, distance):
    n = lax.axis_size(axis)
    route = [(i, i + distance) for i in range(n) if 0 <= i + distance < n]
    return lax.ppermute(value, axis, route)


def step(valence, start, tiles, home, ox, oy, oz, size):
    place = jnp.stack([lax.axis_index(DOM), lax.axis_index(GRP)]).astype(I32)
    lower = shift(start[CX - HU :], DOM, 1)
    upper = shift(start[:HU], DOM, -1)
    message = pack_atoms([v.reshape(-1) for v in (home, ox, oy, oz, size)], tiles)
    got = lax.all_to_all(message.reshape(NDEV, ROWS * LANES), ALL, 0, 0, tiled=True)
    got = got.reshape(NDEV * ROWS, LANES)
    u_left, u_right = edges(*own_edges(start), lower, upper)
    grid, up2, down = deposit(got, valence)
    from1 = shift(grid[2 * CY : 15 * CY].reshape(13, CY, LANES), DOM, 1)
    from2 = shift(up2.reshape(5, CY, LANES), DOM, 2)
    above = shift(down.reshape(6, CY, LANES), DOM, -1)
    u_from_right = shift(u_left, GRP, -1)
    u_from_left = shift(u_right, GRP, 1)
    f, left, right = join(
        grid, from1, from2, above
    )
    from_right = shift(left, GRP, -1)
    from_left = shift(right, GRP, 1)
    u2, fe, f1, chunk = before(
        place, f, lower, start, upper, u_from_left, u_from_right, from_left, from_right
    )
    f1_lo = shift(f1[1:4], DOM, 1)
    f1_hi = shift(f1[4:7], DOM, -1)
    chunks = jnp.broadcast_to(chunk[None], (NDEV, 8, LANES))
    everything = lax.all_to_all(chunks, ALL, 0, 0, tiled=True)
    potential, totals = after(place, everything, f1, f1_lo, f1_hi, u2, fe)
    sums = lax.all_to_all(totals, ALL, 0, 0, tiled=True)
    return potential, stress_of(sums)


def solution(mesh):
    split = Mesh(mesh.devices.reshape(4, 4, 4, 2), ("dom_0", "dom_1", "grp_0", "grp_1"))
    atoms = P(DOM + GRP, None)
    return jax.shard_map(
        step,
        mesh=split,
        in_specs=(P(DOM, None, GRP), P(DOM, None, GRP)) + (atoms,) * 6,
        out_specs=(P(DOM, None, GRP), P()),
        check_vma=False,
    )
```
